512 devices in a mesh: dp: 64 (over y, z_hi, core), expert: 8 (over x, z_lo).
Axes of the slice: x: 4, y: 8, z: 8 (z_hi: 4, z_lo: 2; z = z_hi * 2 + z_lo), core: 2. Of those that a mesh axis runs over, the one named last changes fastest.
Arguments:
- activations: bfloat16 [4096, 4096], P('expert', 'dp'), may hold values from -6 to 6
- out_grad: bfloat16 [4096, 4096], P('expert', 'dp'), may hold values from -6 to 6
- w_in: bfloat16 [8, 4096, 8192], P('expert', None, 'dp'), may hold values from -0.25 to 0.25
- w_out: bfloat16 [8, 8192, 4096], P('expert', 'dp'), may hold values from -0.0625 to 0.0625
- chosen: int32 [8, 256], replicated, may hold values from 0 to 4095, as said below
- gate_scores: float32 [8, 256], P('expert'), may hold values from 0.2 to 1
Outputs:
- w_in_grad: bfloat16 [8, 4096, 8192], P('expert', None, 'dp')
- w_out_grad: bfloat16 [8, 8192, 4096], P('expert', 'dp')
- act_grad: bfloat16 [4096, 4096], P('expert', 'dp')
- gate_grad: float32 [8, 256], P('expert')
The draws below stay inside these ranges and needn't reach their ends.
Inputs may be any that keep to these rules, and one draw needn't show every extreme that they name: Each row of chosen holds 256 distinct token numbers.
All inputs are finite; a program needn't handle non-finite values.
Results may differ from the reference program's by a relative error of at most 0.0075.
Values may be sent and summed in bfloat16 or wider, within the bound.
No kernel may reach another device: no remote copies, remote signals or barrier semaphores. Data moves between devices by JAX's collectives and lax.ppermute only.
A program may use at most 64 MiB of HBM per device.

```python
import jax
import jax.numpy as jnp

D = 4096
FF = 8192
ROWS = 256
EXPERTS = 8
TOKENS = 4096


def draw_chosen(key, part):
    expert_keys = jax.random.split(key, EXPERTS)

    def one_list(expert_key):
        return jax.random.permutation(expert_key, TOKENS)[:ROWS]
    return jax.vmap(one_list)(expert_keys).astype(jnp.int32)


def spiked(array, key, source, target, blocks, factor):
    owner, partner = [(jnp.arange(array.shape[position]) // (array.shape[position] // blocks)).reshape([-1 if axis == position else 1 for axis in range(array.ndim)]) for position in (source, target)]
    chosen = jax.random.permutation(key, blocks)[partner]
    strong = (owner == chosen) | (owner == (partner + blocks // 2) % blocks)
    return jnp.where(strong, factor * array, array)


def block_scale(own_key, extent, shards, low, largest):
    def one(dim, parts):
        steps = jax.random.uniform(jax.random.fold_in(jax.random.fold_in(own_key, 6), dim), (parts,), jnp.float32, low / len(shards), largest / len(shards))
        return jnp.repeat(jnp.exp(steps), extent[dim] // parts).reshape((-1,) + (1,) * (len(extent) - dim - 1))

    factor_of = one(*shards[0])
    for cut in shards[1:]:
        factor_of = factor_of * one(*cut)
    return factor_of


def bell_draw(key, dims, width, reach, cuts=(), dtype=jnp.bfloat16):
    drawn = width * jax.random.normal(key, dims, jnp.float32)
    if cuts:
        drawn = drawn * block_scale(key, dims, cuts, -0.22, 0.18)
    return jnp.clip(drawn, -reach, reach).astype(dtype)


def heavy_noise(own_key, extent, spread, reach, cuts, heavy, held_as=jnp.bfloat16):
    result = spread * jax.random.normal(own_key, extent, jnp.float32)
    if cuts:
        result = result * block_scale(own_key, extent, cuts, -0.22, 0.18)
    return jnp.clip(spiked(result, jax.random.fold_in(own_key, 3), *heavy), -reach, reach).astype(held_as)


def setup_inputs(seed: int = 0) -> dict:
    key_list = jax.random.split(jax.random.key(seed), 7)
    return {
        "activations": bell_draw(key_list[0], (TOKENS, D), 1.0, 6.0, ((0, 8), (1, 64))),
        "out_grad": bell_draw(key_list[1], (TOKENS, D), 1.0, 6.0, ((0, 8), (1, 64))),
        "w_in": heavy_noise(key_list[2], (EXPERTS, D, FF), D ** -0.5, 0.25, ((0, 8), (2, 64)), (2, 1, 64, 4.0)),
        "w_out": bell_draw(key_list[3], (EXPERTS, FF, D), FF ** -0.5, 0.0625, ((0, 8), (1, 64))),
        "chosen": draw_chosen(jax.random.fold_in(key_list[6], 71), 0),
        "gate_scores": jnp.clip(0.2 + 0.8 * jax.random.uniform(key_list[5], (EXPERTS, ROWS), jnp.float32) ** block_scale(key_list[5], (EXPERTS, ROWS), ((0, 8),), -0.2, 0.2), 0.2, 1.0),
    }


GELU_SCALE = 0.7978845608
CUBIC_COEF = 0.044715


def gelu_parts(preact):
    inner = GELU_SCALE * (preact + CUBIC_COEF * preact * preact * preact)
    tanh_part = jnp.tanh(inner)
    gelu_val = 0.5 * preact * (1.0 + tanh_part)
    gelu_slope = 0.5 * (1.0 + tanh_part) + 0.5 * preact * (1.0 - tanh_part * tanh_part) * GELU_SCALE * (1.0 + 3.0 * CUBIC_COEF * preact * preact)
    return gelu_val, gelu_slope


def reference(activations, out_grad, w_in, w_out, chosen, gate_scores):
    act_total = jnp.zeros(activations.shape, jnp.float32)
    in_grads = []
    out_grads = []
    gate_rows = []
    for expert_id in range(EXPERTS):
        picked = chosen[expert_id].astype(jnp.int32)
        inputs = jnp.take(activations, picked, axis=0)
        upstream = jnp.take(out_grad, picked, axis=0)
        gated_grad = (gate_scores[expert_id][:, None] * upstream.astype(jnp.float32)).astype(jnp.bfloat16)
        preact = jnp.dot(inputs, w_in[expert_id], preferred_element_type=jnp.float32)
        gelu_val, gelu_slope = gelu_parts(preact)
        hidden = gelu_val.astype(jnp.bfloat16)
        raw_back = jnp.dot(upstream, w_out[expert_id].T, preferred_element_type=jnp.float32)
        gate_rows.append(jnp.sum(hidden.astype(jnp.float32) * raw_back, axis=1))
        hidden_back = jnp.dot(gated_grad, w_out[expert_id].T, preferred_element_type=jnp.float32)
        preact_back = (hidden_back * gelu_slope).astype(jnp.bfloat16)
        out_grads.append(jnp.dot(hidden.T, gated_grad, preferred_element_type=jnp.float32).astype(jnp.bfloat16))
        in_grads.append(jnp.dot(inputs.T, preact_back, preferred_element_type=jnp.float32).astype(jnp.bfloat16))
        input_back = jnp.dot(preact_back, w_in[expert_id].T, preferred_element_type=jnp.float32)
        act_total = act_total.at[picked].add(input_back)
    return (jnp.stack(in_grads), jnp.stack(out_grads), act_total.astype(jnp.bfloat16), jnp.stack(gate_rows))
```

```python
import jax
import jax.numpy as jnp
import numpy as np
from jax import lax
from jax.experimental import pallas as pl
from jax.experimental.pallas import tpu as pltpu
from jax.sharding import PartitionSpec as P

GELU_SCALE = 0.7978845608
CUBIC_COEF = 0.044715

NY, NZ = 8, 4
NQ = NY // 2
VMEM_BYTES = 48 * 1024 * 1024
BF, F32 = jnp.bfloat16, jnp.float32


def dp_index(y, z, core):
    return (y * NZ + z) * 2 + core


INNER = [[dp_index(y, z, 0) for y in range(NY)] for z in range(NZ)] + [
    [dp_index(2 * q + p, z, 1) for p in range(2) for z in range(NZ)] for q in range(NQ)
]
OUTER = [[dp_index(y, z, 0) for z in range(NZ)] for y in range(NY)] + [
    [dp_index(2 * q + p, z, 1) for q in range(NQ)] for p in range(2) for z in range(NZ)
]
SWAP = [(d, d ^ 1) for d in range(NY * NZ * 2)]
SLOTS = [
    np.array([dp_index(i, o, 0) for o in range(NZ) for i in range(NY)], np.int32),
    np.array(
        [dp_index(2 * o + i // NZ, i % NZ, 1) for o in range(NQ) for i in range(8)],
        np.int32,
    ),
]


def gelu_parts(preact):
    inner = GELU_SCALE * (preact + CUBIC_COEF * preact * preact * preact)
    tanh_part = jnp.tanh(inner)
    gelu_val = 0.5 * preact * (1.0 + tanh_part)
    gelu_slope = 0.5 * (1.0 + tanh_part) + 0.5 * preact * (
        1.0 - tanh_part * tanh_part
    ) * GELU_SCALE * (1.0 + 3.0 * CUBIC_COEF * preact * preact)
    return gelu_val, gelu_slope


def contract(left, right, left_axis, right_axis):
    return lax.dot_general(
        left, right, (((left_axis,), (right_axis,)), ((), ())), preferred_element_type=F32
    )


def onehot(base, chosen_row, tokens):
    rows = chosen_row.shape[1]
    ids = base + lax.broadcasted_iota(jnp.int32, (tokens, rows), 0)
    return jnp.where(ids == chosen_row, 1.0, 0.0).astype(BF)


def hi_lo(value):
    high = value.astype(BF)
    low = (value - high.astype(F32)).astype(BF)
    return high, low


def pick_kernel(base_ref, act_ref, grad_ref, chosen_ref, out_ref):
    both = jnp.concatenate([act_ref[...], grad_ref[...]], axis=0)
    for e in range(out_ref.shape[0]):
        sel = onehot(base_ref[0], chosen_ref[e : e + 1, :], both.shape[1])
        out_ref[e] = contract(both, sel, 1, 0).astype(BF)


def merge_kernel(parts_ref, out_ref):
    total = parts_ref[0].astype(F32)
    for k in range(1, parts_ref.shape[0]):
        total = total + parts_ref[k].astype(F32)
    total = total.astype(BF)
    for k in range(out_ref.shape[0]):
        out_ref[k] = total


def main_kernel(
    slots_ref, own_ref, oth_ref, w_in_ref, w_out_ref, score_ref,
    gin_ref, gout_ref, keep_ref, send_ref, x_ref, u_ref,
):
    feats = own_ref.shape[2] // 2
    slots = own_ref.shape[0] * own_ref.shape[1]
    for half, ref in enumerate((own_ref, oth_ref)):
        for s in range(slots):
            at = pl.ds(pl.multiple_of(slots_ref[half * slots + s] * feats, feats), feats)
            o, i = s // ref.shape[1], s % ref.shape[1]
            x_ref[at, :] = ref[o, i, :feats, :]
            u_ref[at, :] = ref[o, i, feats:, :]
    preact = contract(w_in_ref[...], x_ref[...], 0, 0)
    raw = contract(w_out_ref[...], u_ref[...], 1, 0)
    val, slope = gelu_parts(preact)
    hidden = val.astype(BF).astype(F32)
    score = score_ref[...]
    gate = jnp.sum(hidden * raw, axis=0, keepdims=True)
    back = (score * raw * slope).astype(BF)
    scaled = (score * hidden).astype(BF)
    for half, ref in enumerate((keep_ref, send_ref)):
        for s in range(slots):
            at = pl.ds(pl.multiple_of(slots_ref[half * slots + s] * feats, feats), feats)
            ref[pl.ds(s * feats, feats), :] = contract(w_in_ref[at, :], back, 1, 0).astype(BF)
        high, low = hi_lo(gate)
        pad = jnp.zeros((14, gate.shape[1]), F32)
        tile = jnp.concatenate([high.astype(F32), low.astype(F32), pad], axis=0)
        ref[pl.ds(slots * feats, 16), :] = tile.astype(BF)
    gin_ref[...] = contract(x_ref[...], back, 1, 1).astype(BF)
    gout_ref[...] = contract(scaled, u_ref[...], 1, 1).astype(BF)


def pair_kernel(keep_ref, got_ref, out_ref):
    parts, rows = out_ref.shape[0], out_ref.shape[1] - 16
    base = parts * rows
    gates = keep_ref[pl.ds(base, 16), :].astype(F32), got_ref[pl.ds(base, 16), :].astype(F32)
    gate = (gates[0][0:1] + gates[0][1:2]) + (gates[1][0:1] + gates[1][1:2])
    high, low = hi_lo(gate)
    pad = jnp.zeros((14, gate.shape[1]), F32)
    tile = jnp.concatenate([high.astype(F32), low.astype(F32), pad], axis=0).astype(BF)
    for k in range(parts):
        at = pl.ds(k * rows, rows)
        out_ref[k, :rows, :] = (keep_ref[at, :].astype(F32) + got_ref[at, :].astype(F32)).astype(BF)
        out_ref[k, rows:, :] = tile


def outer_kernel(got_ref, out_ref):
    parts, rows = out_ref.shape[0], out_ref.shape[1] - 16
    sources, base = got_ref.shape[0], parts * rows
    gates = [got_ref[o, pl.ds(base, 16), :].astype(F32)[0:2] for o in range(sources)]
    pad = jnp.zeros((16 - 2 * sources, got_ref.shape[2]), F32)
    tile = jnp.concatenate(gates + [pad], axis=0).astype(BF)
    for k in range(parts):
        at = pl.ds(k * rows, rows)
        total = got_ref[0, at, :].astype(F32)
        for o in range(1, sources):
            total = total + got_ref[o, at, :].astype(F32)
        out_ref[k, :rows, :] = total.astype(BF)
        out_ref[k, rows:, :] = tile


def inner_kernel(core_ref, got_ref, out_ref, gate_ref):
    rows = out_ref.shape[1]
    sources = got_ref.shape[0]
    total = got_ref[0, :rows, :].astype(F32)
    for i in range(1, sources):
        total = total + got_ref[i, :rows, :].astype(F32)
    total = total.astype(BF)
    for k in range(out_ref.shape[0]):
        out_ref[k] = total
    tiles = [got_ref[i, rows:, :].astype(F32) for i in range(sources)]
    gates = [[t[2 * o : 2 * o + 1] + t[2 * o + 1 : 2 * o + 2] for o in range(NZ)] for t in tiles]
    first = core_ref[0] == 0
    gate = jnp.zeros((1, got_ref.shape[2]), F32)
    for y in range(NY):
        for z in range(NZ):
            gate = gate + jnp.where(first, gates[y][z], gates[(y % 2) * NZ + z][y // 2])
    gate_ref[...] = gate


def scatter_kernel(base_ref, terms_ref, chosen_ref, out_ref):
    tokens = out_ref.shape[1]
    total = jnp.zeros(out_ref.shape, F32)
    for e in range(terms_ref.shape[0]):
        sel = onehot(base_ref[0], chosen_ref[e : e + 1, :], tokens)
        total = total + contract(terms_ref[e], sel, 1, 1)
    out_ref[...] = total.astype(BF)


SMEM = pl.BlockSpec(memory_space=pltpu.SMEM)
VMEM = pl.BlockSpec(memory_space=pltpu.VMEM)


def call(kernel, specs, outs, *args, scratch=()):
    shapes = [jax.ShapeDtypeStruct(s, t) for s, t in outs]
    single = len(shapes) == 1
    return pl.pallas_call(
        kernel,
        out_shape=shapes[0] if single else shapes,
        in_specs=specs,
        out_specs=VMEM if single else [VMEM] * len(shapes),
        scratch_shapes=scratch,
        compiler_params=pltpu.CompilerParams(vmem_limit_bytes=VMEM_BYTES),
    )(*args)


def exchange(parts, axis, groups=None):
    return lax.all_to_all(parts, axis, 0, 0, axis_index_groups=groups)


def per_device(activations, out_grad, w_in, w_out, chosen, gate_scores):
    tokens, feats = activations.shape
    experts, rows = chosen.shape
    depth, units = w_in.shape[1], w_in.shape[2]
    base = (lax.axis_index("expert") * tokens).astype(jnp.int32).reshape(1)
    core = (lax.axis_index("dp") % 2).astype(jnp.int32).reshape(1)
    own = jnp.where(core == 0, jnp.asarray(SLOTS[0]), jnp.asarray(SLOTS[1]))
    oth = jnp.where(core == 0, jnp.asarray(SLOTS[1]), jnp.asarray(SLOTS[0]))
    slots = jnp.concatenate([own, oth])
    count = own.shape[0]

    picked = call(
        pick_kernel, [SMEM, VMEM, VMEM, VMEM], [((experts, 2 * feats, rows), BF)],
        base, activations.T, out_grad.T, chosen,
    )
    picked = exchange(picked, "expert")
    mine = call(merge_kernel, [VMEM], [((8, 2 * feats, rows), BF)], picked)
    inner = exchange(mine, "dp", INNER)
    outer = exchange(jnp.broadcast_to(inner[None], (4,) + inner.shape), "dp", OUTER)
    other = lax.ppermute(outer, "dp", SWAP)

    weight_in_grad, weight_out_grad, keep, send = call(
        main_kernel,
        [SMEM, VMEM, VMEM, VMEM, VMEM, VMEM],
        [
            ((depth, units), BF),
            ((units, depth), BF),
            ((count * feats + 16, rows), BF),
            ((count * feats + 16, rows), BF),
        ],
        slots, outer, other, w_in[0], w_out[0], gate_scores,
        scratch=[pltpu.VMEM((depth, rows), BF), pltpu.VMEM((depth, rows), BF)],
    )
    got = lax.ppermute(send, "dp", SWAP)
    part = call(pair_kernel, [VMEM, VMEM], [((4, 8 * feats + 16, rows), BF)], keep, got)
    part = exchange(part, "dp", OUTER)
    part = call(outer_kernel, [VMEM], [((8, feats + 16, rows), BF)], part)
    part = exchange(part, "dp", INNER)
    term, gate_grad = call(
        inner_kernel, [SMEM, VMEM], [((experts, feats, rows), BF), ((1, rows), F32)], core, part
    )
    terms = exchange(term, "expert")
    act_grad = call(
        scatter_kernel, [SMEM, VMEM, VMEM], [((feats, tokens), BF)], base, terms, chosen
    )
    return weight_in_grad[None], weight_out_grad[None], act_grad.T, gate_grad


def solution(mesh):
    return jax.shard_map(
        per_device,
        mesh=mesh,
        in_specs=(
            P("expert", "dp"),
            P("expert", "dp"),
            P("expert", None, "dp"),
            P("expert", "dp", None),
            P(),
            P("expert", None),
        ),
        out_specs=(
            P("expert", None, "dp"),
            P("expert", "dp", None),
            P("expert", "dp"),
            P("expert", None),
        ),
        check_vma=False,
    )
```

```python
import jax
import jax.numpy as jnp
from jax import lax
from jax.experimental import pallas as pl
from jax.experimental.pallas import tpu as pltpu
from jax.sharding import PartitionSpec as P

GELU_SCALE = 0.7978845608
CUBIC_COEF = 0.044715

NY, NZ = 8, 4
MIB = 1024 * 1024
BF, F32 = jnp.bfloat16, jnp.float32


def dp_index(y, z, core):
    return (y * NZ + z) * 2 + core


INNER = [[dp_index(y, z, 0) for y in range(NY)] for z in range(NZ)] + [
    [dp_index(4 * h + q, z, 1) for h in range(2) for z in range(NZ)] for q in range(4)
]
OUTER = [[dp_index(y, z, 0) for z in range(NZ)] for y in range(NY)] + [
    [dp_index(4 * h + q, z, 1) for q in range(4)] for h in range(2) for z in range(NZ)
]
SHIFTS = [
    [(g[j], g[(j + k) % 4]) for g in OUTER for j in range(4)] for k in range(4)
]
SWAP = [(d, d ^ 1) for d in range(NY * NZ * 2)]


def gelu_parts(preact):
    inner = GELU_SCALE * (preact + CUBIC_COEF * preact * preact * preact)
    tanh_part = jnp.tanh(inner)
    gelu_val = 0.5 * preact * (1.0 + tanh_part)
    gelu_slope = 0.5 * (1.0 + tanh_part) + 0.5 * preact * (
        1.0 - tanh_part * tanh_part
    ) * GELU_SCALE * (1.0 + 3.0 * CUBIC_COEF * preact * preact)
    return gelu_val, gelu_slope


def contract(left, right, left_axis, right_axis):
    return lax.dot_general(
        left, right, (((left_axis,), (right_axis,)), ((), ())), preferred_element_type=F32
    )


def onehot(base, chosen_row, tokens):
    rows = chosen_row.shape[1]
    ids = base + lax.broadcasted_iota(jnp.int32, (tokens, rows), 0)
    return jnp.where(ids == chosen_row, 1.0, 0.0).astype(BF)


def hi_lo(value):
    high = value.astype(BF)
    low = (value - high.astype(F32)).astype(BF)
    return high, low


def pick_kernel(
    base_ref, act_hbm, grad_hbm, chosen_hbm, out_ref, sel_ref, both_ref, chosen_ref, sems
):
    feats = act_hbm.shape[0]
    copies = [
        pltpu.make_async_copy(act_hbm, both_ref.at[pl.ds(0, feats)], sems.at[0]),
        pltpu.make_async_copy(grad_hbm, both_ref.at[pl.ds(feats, feats)], sems.at[1]),
        pltpu.make_async_copy(chosen_hbm, chosen_ref, sems.at[2]),
    ]
    for copy in copies:
        copy.start()
    for copy in copies:
        copy.wait()
    both = both_ref[...]
    for e in range(out_ref.shape[0]):
        sel = onehot(base_ref[0], chosen_ref[e : e + 1, :], both.shape[1])
        sel_ref[e] = sel
        out_ref[e] = contract(both, sel, 1, 0).astype(BF)


def merge_kernel(parts_ref, out_ref):
    total = parts_ref[0].astype(F32)
    for k in range(1, parts_ref.shape[0]):
        total = total + parts_ref[k].astype(F32)
    total = total.astype(BF)
    for k in range(out_ref.shape[0]):
        out_ref[k] = total


def gate_tile(pairs):
    rows = [half.astype(F32) for pair in pairs for half in pair]
    rows.append(jnp.zeros((16 - len(rows), rows[0].shape[1]), F32))
    return jnp.concatenate(rows, axis=0).astype(BF)


def block_rows(slots_ref, slot, feats):
    return pl.ds(pl.multiple_of(slots_ref[slot] * feats, feats), feats)


def main_kernel(slots_ref, *refs):
    parts, (w_in_ref, w_out_ref, score_ref) = refs[:8], refs[8:11]
    x_ref, u_ref, back_ref, scaled_ref, gate_ref, send_ref = refs[11:17]
    w_out_held, x_sem, u_sem, w_sem = refs[17:]
    weights = pltpu.make_async_copy(w_out_ref, w_out_held, w_sem)
    inner, feats = parts[0].shape[0], parts[0].shape[1] // 2
    for k, ref in enumerate(parts):
        for i in range(inner):
            at = block_rows(slots_ref, k * inner + i, feats)
            pltpu.make_async_copy(ref.at[i, pl.ds(0, feats)], x_ref.at[at], x_sem).start()
            pltpu.make_async_copy(ref.at[i, pl.ds(feats, feats)], u_ref.at[at], u_sem).start()
    weights.start()
    pltpu.make_async_copy(x_ref, x_ref, x_sem).wait()
    preact = contract(w_in_ref[...], x_ref[...], 0, 0)
    pltpu.make_async_copy(u_ref, u_ref, u_sem).wait()
    weights.wait()
    raw = contract(w_out_held[...], u_ref[...], 1, 0)
    val, slope = gelu_parts(preact)
    hidden = val.astype(BF).astype(F32)
    score = score_ref[...]
    gate = jnp.sum(hidden * raw, axis=0, keepdims=True)
    back = (score * raw * slope).astype(BF)
    back_ref[...] = back
    scaled_ref[...] = (score * hidden).astype(BF)
    gate_ref[...] = gate
    count = send_ref.shape[0] // feats
    for s in range(count):
        at = block_rows(slots_ref, 8 * inner + s, feats)
        send_ref[pl.ds(s * feats, feats), :] = contract(w_in_ref[at, :], back, 1, 0).astype(BF)
    send_ref[pl.ds(count * feats, 16), :] = gate_tile([hi_lo(gate)])


def weight_kernel(x_ref, u_ref, back_ref, scaled_ref, gin_ref, gout_ref):
    gin_ref[...] = contract(x_ref[...], back_ref[...], 1, 1).astype(BF)
    gout_ref[...] = contract(scaled_ref[...], u_ref[...], 1, 1).astype(BF)


def pair_kernel(slots_ref, w_in_ref, back_ref, gate_ref, got_ref, *outs):
    rows = outs[0].shape[0] - 16
    feats = rows // 8
    tile = got_ref[pl.ds(len(outs) * rows, 16), :].astype(F32)
    high, low = hi_lo(gate_ref[...])
    gate = (high.astype(F32) + low.astype(F32)) + (tile[0:1] + tile[1:2])
    packed = gate_tile([hi_lo(gate)])
    back = back_ref[...]
    for k, ref in enumerate(outs):
        for i in range(8):
            s = k * 8 + i
            mine = contract(w_in_ref[block_rows(slots_ref, s, feats), :], back, 1, 0)
            other = got_ref[pl.ds(s * feats, feats), :].astype(F32)
            ref[pl.ds(i * feats, feats), :] = (mine + other).astype(BF)
        ref[pl.ds(rows, 16), :] = packed


def outer_kernel(place_ref, *refs):
    parts, out_ref = refs[:4], refs[4]
    count, rows = out_ref.shape[0], out_ref.shape[1] - 16
    base = count * rows
    tiles = [ref[pl.ds(base, 16), :].astype(F32) for ref in parts]
    pairs = []
    for o in range(4):
        source = (place_ref[0] + 4 - o) % 4
        pair = tiles[0]
        for k in range(1, 4):
            pair = jnp.where(source == k, tiles[k], pair)
        pairs.append((pair[0:1], pair[1:2]))
    packed = gate_tile(pairs)
    for i in range(count):
        at = pl.ds(i * rows, rows)
        total = parts[0][at, :].astype(F32)
        for k in range(1, 4):
            total = total + parts[k][at, :].astype(F32)
        out_ref[i, :rows, :] = total.astype(BF)
        out_ref[i, rows:, :] = packed


def inner_kernel(core_ref, got_ref, out_ref, gate_ref):
    rows = out_ref.shape[1]
    sources = got_ref.shape[0]
    total = got_ref[0, :rows, :].astype(F32)
    for i in range(1, sources):
        total = total + got_ref[i, :rows, :].astype(F32)
    total = total.astype(BF)
    for k in range(out_ref.shape[0]):
        out_ref[k] = total
    tiles = [got_ref[i, rows:, :].astype(F32) for i in range(sources)]
    gates = [[t[2 * o : 2 * o + 1] + t[2 * o + 1 : 2 * o + 2] for o in range(4)] for t in tiles]
    first = core_ref[0] == 0
    gate = jnp.zeros((1, got_ref.shape[2]), F32)
    for y in range(NY):
        for z in range(NZ):
            gate = gate + jnp.where(first, gates[y][z], gates[(y // 4) * NZ + z][y % 4])
    gate_ref[...] = gate


def scatter_kernel(terms_ref, sel_ref, out_ref):
    total = jnp.zeros(out_ref.shape, F32)
    for e in range(terms_ref.shape[0]):
        total = total + contract(terms_ref[e], sel_ref[e], 1, 1)
    out_ref[...] = total.astype(BF)


SMEM = pl.BlockSpec(memory_space=pltpu.SMEM)
VMEM = pl.BlockSpec(memory_space=pltpu.VMEM)
HBM = pl.BlockSpec(memory_space=pltpu.HBM)


def call(kernel, specs, outs, *args, scratch=(), mib=16, flops=0, moved=0):
    shapes = [jax.ShapeDtypeStruct(s, t) for s, t in outs]
    single = len(shapes) == 1
    return pl.pallas_call(
        kernel,
        out_shape=shapes[0] if single else shapes,
        in_specs=specs,
        out_specs=VMEM if single else [VMEM] * len(shapes),
        scratch_shapes=scratch,
        cost_estimate=pl.CostEstimate(flops=flops, bytes_accessed=moved, transcendentals=0),
        compiler_params=pltpu.CompilerParams(vmem_limit_bytes=mib * MIB),
    )(*args)


def in_hbm(value):
    return pltpu.with_memory_space_constraint(value, pltpu.HBM)


def exchange(parts, axis, groups=None):
    return lax.all_to_all(parts, axis, 0, 0, axis_index_groups=groups)


def block_table(core, place):
    o = place[:, None]
    i = jnp.arange(8, dtype=jnp.int32)[None, :]
    zero = dp_index(i, o, 0)
    one = dp_index(4 * (i // NZ) + o, i % NZ, 1)
    return jnp.where(core == 0, zero, one).reshape(-1)


def per_device(activations, out_grad, w_in, w_out, chosen, gate_scores):
    tokens, feats = activations.shape
    experts, rows = chosen.shape
    depth, units = w_in.shape[1], w_in.shape[2]
    base = (lax.axis_index("expert") * tokens).astype(jnp.int32).reshape(1)
    index = lax.axis_index("dp").astype(jnp.int32)
    core, z, y = index & 1, (index >> 1) & (NZ - 1), index >> 3
    place = jnp.where(core == 0, z, y & 3)
    other_place = jnp.where(core == 0, y & 3, z)
    steps = jnp.arange(4, dtype=jnp.int32)
    gathered = jnp.concatenate(
        [
            block_table(core, (place - steps) & 3),
            block_table(1 - core, (other_place - steps) & 3),
            block_table(1 - core, (other_place + steps) & 3),
        ]
    )
    summed = block_table(core, (place + steps) & 3)
    count = summed.shape[0]

    picked, sel = call(
        pick_kernel,
        [SMEM, HBM, HBM, HBM],
        [((experts, 2 * feats, rows), BF), ((experts, tokens, rows), BF)],
        base, in_hbm(activations.T), in_hbm(out_grad.T), in_hbm(chosen),
        scratch=[
            pltpu.VMEM((2 * feats, tokens), BF),
            pltpu.VMEM((experts, rows), jnp.int32),
            pltpu.SemaphoreType.DMA((3,)),
        ],
    )
    picked = exchange(picked, "expert")
    mine = call(merge_kernel, [VMEM], [((8, 2 * feats, rows), BF)], picked)
    own = exchange(mine, "dp", INNER)
    blocks = [own] + [lax.ppermute(own, "dp", SHIFTS[k]) for k in (1, 2, 3)]
    blocks += [lax.ppermute(block, "dp", SWAP) for block in blocks]

    x, u, back, scaled, gate, send = call(
        main_kernel,
        [SMEM] + [HBM] * 8 + [VMEM, HBM, VMEM],
        [
            ((depth, rows), BF),
            ((depth, rows), BF),
            ((units, rows), BF),
            ((units, rows), BF),
            ((1, rows), F32),
            ((count * feats + 16, rows), BF),
        ],
        gathered, *blocks, w_in[0], in_hbm(w_out[0]), gate_scores, mib=24,
        scratch=[pltpu.VMEM((units, depth), BF)] + [pltpu.SemaphoreType.DMA] * 3,
    )
    got = lax.ppermute(send, "dp", SWAP)
    weight_in_grad, weight_out_grad = call(
        weight_kernel,
        [VMEM] * 4,
        [((depth, units), BF), ((units, depth), BF)],
        x, u, back, scaled, flops=4 * depth * units * rows, moved=6 * depth * rows,
    )
    parts = call(
        pair_kernel,
        [SMEM] + [VMEM] * 4,
        [((8 * feats + 16, rows), BF)] * 4,
        summed, w_in[0], back, gate, got,
    )
    parts = [parts[0]] + [lax.ppermute(parts[k], "dp", SHIFTS[k]) for k in (1, 2, 3)]
    part = call(
        outer_kernel, [SMEM] + [VMEM] * 4, [((8, feats + 16, rows), BF)],
        place.reshape(1), *parts,
    )
    part = exchange(part, "dp", INNER)
    term, gate_grad = call(
        inner_kernel, [SMEM, VMEM], [((experts, feats, rows), BF), ((1, rows), F32)],
        core.reshape(1), part,
    )
    terms = exchange(term, "expert")
    act_grad = call(scatter_kernel, [VMEM, VMEM], [((feats, tokens), BF)], terms, sel)
    return weight_in_grad[None], weight_out_grad[None], act_grad.T, gate_grad


def solution(mesh):
    return jax.shard_map(
        per_device,
        mesh=mesh,
        in_specs=(
            P("expert", "dp"),
            P("expert", "dp"),
            P("expert", None, "dp"),
            P("expert", "dp", None),
            P(),
            P("expert", None),
        ),
        out_specs=(
            P("expert", None, "dp"),
            P("expert", "dp", None),
            P("expert", "dp"),
            P("expert", None),
        ),
        check_vma=False,
    )
```

```python
import jax
import jax.numpy as jnp
from jax import lax
from jax.experimental import pallas as pl
from jax.experimental.pallas import tpu as pltpu
from jax.sharding import PartitionSpec as P

GELU_SCALE = 0.7978845608
CUBIC_COEF = 0.044715

NY, NZ = 8, 4
MIB = 1024 * 1024
BF, F32 = jnp.bfloat16, jnp.float32


def dp_index(y, z, core):
    return (y * NZ + z) * 2 + core


INNER = [[dp_index(y, z, 0) for y in range(NY)] for z in range(NZ)] + [
    [dp_index(4 * h + q, z, 1) for h in range(2) for z in range(NZ)] for q in range(4)
]
OUTER = [[dp_index(y, z, 0) for z in range(NZ)] for y in range(NY)] + [
    [dp_index(4 * h + q, z, 1) for q in range(4)] for h in range(2) for z in range(NZ)
]
SWAP = [(d, d ^ 1) for d in range(NY * NZ * 2)]


def gelu_parts(preact):
    inner = GELU_SCALE * (preact + CUBIC_COEF * preact * preact * preact)
    tanh_part = jnp.tanh(inner)
    gelu_val = 0.5 * preact * (1.0 + tanh_part)
    gelu_slope = 0.5 * (1.0 + tanh_part) + 0.5 * preact * (
        1.0 - tanh_part * tanh_part
    ) * GELU_SCALE * (1.0 + 3.0 * CUBIC_COEF * preact * preact)
    return gelu_val, gelu_slope


def contract(left, right, left_axis, right_axis):
    return lax.dot_general(
        left, right, (((left_axis,), (right_axis,)), ((), ())), preferred_element_type=F32
    )


def onehot(base, chosen_row, tokens):
    rows = chosen_row.shape[1]
    ids = base + lax.broadcasted_iota(jnp.int32, (tokens, rows), 0)
    return jnp.where(ids == chosen_row, 1.0, 0.0).astype(BF)


def hi_lo(value):
    high = value.astype(BF)
    low = (value - high.astype(F32)).astype(BF)
    return high, low


def pick_kernel(
    base_ref, act_hbm, grad_hbm, chosen_hbm, out_ref, sel_ref, both_ref, chosen_ref, sems
):
    feats = act_hbm.shape[0]
    copies = [
        pltpu.make_async_copy(act_hbm, both_ref.at[pl.ds(0, feats)], sems.at[0]),
        pltpu.make_async_copy(grad_hbm, both_ref.at[pl.ds(feats, feats)], sems.at[1]),
        pltpu.make_async_copy(chosen_hbm, chosen_ref, sems.at[2]),
    ]
    for copy in copies:
        copy.start()
    for copy in copies:
        copy.wait()
    both = both_ref[...]
    for e in range(out_ref.shape[0]):
        sel = onehot(base_ref[0], chosen_ref[e : e + 1, :], both.shape[1])
        sel_ref[e] = sel
        out_ref[e] = contract(both, sel, 1, 0).astype(BF)


def merge_kernel(parts_ref, out_ref):
    total = parts_ref[0].astype(F32)
    for k in range(1, parts_ref.shape[0]):
        total = total + parts_ref[k].astype(F32)
    total = total.astype(BF)
    for k in range(out_ref.shape[0]):
        out_ref[k] = total


def gate_tile(pairs):
    rows = [half.astype(F32) for pair in pairs for half in pair]
    rows.append(jnp.zeros((16 - len(rows), rows[0].shape[1]), F32))
    return jnp.concatenate(rows, axis=0).astype(BF)


def block_rows(slots_ref, slot, feats):
    return pl.ds(pl.multiple_of(slots_ref[slot] * feats, feats), feats)


def load_blocks(slots_ref, first, blocks_ref, x_ref, u_ref, x_sem, u_sem):
    outer, inner, both = blocks_ref.shape[:3]
    feats = both // 2
    for o in range(outer):
        for i in range(inner):
            at = block_rows(slots_ref, first + o * inner + i, feats)
            act, grad = (blocks_ref.at[o, i, pl.ds(h * feats, feats)] for h in range(2))
            pltpu.make_async_copy(act, x_ref.at[at], x_sem).start()
            pltpu.make_async_copy(grad, u_ref.at[at], u_sem).start()
    half = pl.ds(0, outer * inner * feats)
    return (
        pltpu.make_async_copy(x_ref.at[half], x_ref.at[half], x_sem),
        pltpu.make_async_copy(u_ref.at[half], u_ref.at[half], u_sem),
    )


def ready_kernel(slots_ref, own_ref, w_in_ref, x_ref, u_ref, turned_ref, x_sem, u_sem):
    arrived = load_blocks(slots_ref, 0, own_ref, x_ref, u_ref, x_sem, u_sem)
    turned_ref[...] = w_in_ref[...].T
    for copy in arrived:
        copy.wait()


def main_kernel(
    slots_ref, oth_ref, x_in, u_in, turned_ref, w_in_ref, w_out_ref, score_ref,
    x_ref, u_ref, back_ref, scaled_ref, gate_ref, send_ref, held_ref, x_sem, u_sem, w_sem,
):
    weights = pltpu.make_async_copy(w_out_ref, held_ref, w_sem)
    weights.start()
    slots = oth_ref.shape[0] * oth_ref.shape[1]
    feats = oth_ref.shape[2] // 2
    x_done, u_done = load_blocks(slots_ref, slots, oth_ref, x_ref, u_ref, x_sem, u_sem)
    x_done.wait()
    preact = contract(turned_ref[...], x_ref[...], 1, 0)
    u_done.wait()
    weights.wait()
    raw = contract(held_ref[...], u_ref[...], 1, 0)
    val, slope = gelu_parts(preact)
    hidden = val.astype(BF).astype(F32)
    score = score_ref[...]
    gate = jnp.sum(hidden * raw, axis=0, keepdims=True)
    back = (score * raw * slope).astype(BF)
    back_ref[...] = back
    scaled_ref[...] = (score * hidden).astype(BF)
    gate_ref[...] = gate
    for s in range(slots):
        at = block_rows(slots_ref, slots + s, feats)
        send_ref[pl.ds(s * feats, feats), :] = contract(w_in_ref[at, :], back, 1, 0).astype(BF)
    send_ref[pl.ds(slots * feats, 16), :] = gate_tile([hi_lo(gate)])


def weight_kernel(x_ref, u_ref, back_ref, scaled_ref, gin_ref, gout_ref):
    gin_ref[...] = contract(x_ref[...], back_ref[...], 1, 1).astype(BF)
    gout_ref[...] = contract(scaled_ref[...], u_ref[...], 1, 1).astype(BF)


def pair_kernel(slots_ref, w_in_ref, back_ref, gate_ref, got_ref, out_ref):
    parts, rows = out_ref.shape[0], out_ref.shape[1] - 16
    feats = rows // 8
    back = back_ref[...]
    tile = got_ref[pl.ds(parts * rows, 16), :].astype(F32)
    high, low = hi_lo(gate_ref[...])
    gate = (high.astype(F32) + low.astype(F32)) + (tile[0:1] + tile[1:2])
    packed = gate_tile([hi_lo(gate)])
    for k in range(parts):
        for i in range(8):
            s = k * 8 + i
            mine = contract(w_in_ref[block_rows(slots_ref, s, feats), :], back, 1, 0)
            other = got_ref[pl.ds(s * feats, feats), :].astype(F32)
            out_ref[k, pl.ds(i * feats, feats), :] = (mine + other).astype(BF)
        out_ref[k, rows:, :] = packed


def outer_kernel(got_ref, out_ref):
    count, rows = out_ref.shape[0], out_ref.shape[1] - 16
    base = count * rows
    tiles = [got_ref[o, pl.ds(base, 16), :].astype(F32) for o in range(4)]
    packed = gate_tile([(t[0:1], t[1:2]) for t in tiles])
    for i in range(count):
        at = pl.ds(i * rows, rows)
        total = got_ref[0, at, :].astype(F32)
        for o in range(1, 4):
            total = total + got_ref[o, at, :].astype(F32)
        out_ref[i, :rows, :] = total.astype(BF)
        out_ref[i, rows:, :] = packed


def inner_kernel(core_ref, got_ref, out_ref, gate_ref):
    rows = out_ref.shape[1]
    sources = got_ref.shape[0]
    total = got_ref[0, :rows, :].astype(F32)
    for i in range(1, sources):
        total = total + got_ref[i, :rows, :].astype(F32)
    total = total.astype(BF)
    for k in range(out_ref.shape[0]):
        out_ref[k] = total
    tiles = [got_ref[i, rows:, :].astype(F32) for i in range(sources)]
    gates = [[t[2 * o : 2 * o + 1] + t[2 * o + 1 : 2 * o + 2] for o in range(4)] for t in tiles]
    first = core_ref[0] == 0
    gate = jnp.zeros((1, got_ref.shape[2]), F32)
    for y in range(NY):
        for z in range(NZ):
            gate = gate + jnp.where(first, gates[y][z], gates[(y // 4) * NZ + z][y % 4])
    gate_ref[...] = gate


def scatter_kernel(terms_ref, sel_ref, out_ref):
    total = jnp.zeros(out_ref.shape, F32)
    for e in range(terms_ref.shape[0]):
        total = total + contract(terms_ref[e], sel_ref[e], 1, 1)
    out_ref[...] = total.astype(BF)


SMEM = pl.BlockSpec(memory_space=pltpu.SMEM)
VMEM = pl.BlockSpec(memory_space=pltpu.VMEM)
HBM = pl.BlockSpec(memory_space=pltpu.HBM)
ANY = pl.BlockSpec(memory_space=pl.ANY)


def call(kernel, specs, outs, *args, scratch=(), alias=None, mib=16, flops=0, moved=0):
    shapes = [jax.ShapeDtypeStruct(s, t) for s, t in outs]
    single = len(shapes) == 1
    return pl.pallas_call(
        kernel,
        out_shape=shapes[0] if single else shapes,
        in_specs=specs,
        out_specs=VMEM if single else [VMEM] * len(shapes),
        scratch_shapes=scratch,
        input_output_aliases=alias or {},
        cost_estimate=pl.CostEstimate(flops=flops, bytes_accessed=moved, transcendentals=0),
        compiler_params=pltpu.CompilerParams(vmem_limit_bytes=mib * MIB),
    )(*args)


def in_hbm(value):
    return pltpu.with_memory_space_constraint(value, pltpu.HBM)


def exchange(parts, axis, groups=None):
    return lax.all_to_all(parts, axis, 0, 0, axis_index_groups=groups)


def block_table(core):
    o = jnp.arange(4, dtype=jnp.int32)[:, None]
    i = jnp.arange(8, dtype=jnp.int32)[None, :]
    zero = dp_index(i, o, 0)
    one = dp_index(4 * (i // NZ) + o, i % NZ, 1)
    return jnp.where(core == 0, zero, one).reshape(-1)


def per_device(activations, out_grad, w_in, w_out, chosen, gate_scores):
    tokens, feats = activations.shape
    experts, rows = chosen.shape
    depth, units = w_in.shape[1], w_in.shape[2]
    base = (lax.axis_index("expert") * tokens).astype(jnp.int32).reshape(1)
    core = lax.axis_index("dp").astype(jnp.int32) & 1
    slots = jnp.concatenate([block_table(core), block_table(1 - core)])
    count = slots.shape[0] // 2

    picked, sel = call(
        pick_kernel,
        [SMEM, HBM, HBM, HBM],
        [((experts, 2 * feats, rows), BF), ((experts, tokens, rows), BF)],
        base, in_hbm(activations.T), in_hbm(out_grad.T), in_hbm(chosen),
        scratch=[
            pltpu.VMEM((2 * feats, tokens), BF),
            pltpu.VMEM((experts, rows), jnp.int32),
            pltpu.SemaphoreType.DMA((3,)),
        ],
    )
    picked = exchange(picked, "expert")
    mine = call(merge_kernel, [VMEM], [((8, 2 * feats, rows), BF)], picked)
    inner = exchange(mine, "dp", INNER)
    own = exchange(jnp.broadcast_to(inner[None], (4,) + inner.shape), "dp", OUTER)
    other = lax.ppermute(own, "dp", SWAP)
    sems = [pltpu.SemaphoreType.DMA] * 2
    held = [((depth, rows), BF), ((depth, rows), BF)]
    x, u, turned = call(
        ready_kernel, [SMEM, ANY, VMEM], held + [((units, depth), BF)], slots, own, w_in[0],
        scratch=sems, flops=2 * MIB, moved=6 * MIB,
    )
    x, u, back, scaled, gate, send = call(
        main_kernel,
        [SMEM, ANY] + [VMEM] * 4 + [HBM, VMEM],
        held
        + [
            ((units, rows), BF),
            ((units, rows), BF),
            ((1, rows), F32),
            ((count * feats + 16, rows), BF),
        ],
        slots, other, x, u, turned, w_in[0], in_hbm(w_out[0]), gate_scores,
        scratch=[pltpu.VMEM((units, depth), BF)] + [pltpu.SemaphoreType.DMA] * 3, alias={2: 0, 3: 1},
    )
    got = lax.ppermute(send, "dp", SWAP)
    weight_grads = call(
        weight_kernel,
        [VMEM] * 4,
        [((depth, units), BF), ((units, depth), BF)],
        x, u, back, scaled, flops=4 * depth * units * rows, moved=6 * depth * rows,
    )
    got, weight_in_grad, weight_out_grad = lax.optimization_barrier((got, *weight_grads))
    part = call(
        pair_kernel,
        [SMEM] + [VMEM] * 4,
        [((4, 8 * feats + 16, rows), BF)],
        slots, w_in[0], back, gate, got,
    )
    part = exchange(part, "dp", OUTER)
    part = call(outer_kernel, [VMEM], [((8, feats + 16, rows), BF)], part)
    part = exchange(part, "dp", INNER)
    term, gate_grad = call(
        inner_kernel, [SMEM, VMEM], [((experts, feats, rows), BF), ((1, rows), F32)],
        core.reshape(1), part,
    )
    terms = exchange(term, "expert")
    act_grad = call(scatter_kernel, [VMEM, VMEM], [((feats, tokens), BF)], terms, sel)
    return weight_in_grad[None], weight_out_grad[None], act_grad.T, gate_grad


def solution(mesh):
    return jax.shard_map(
        per_device,
        mesh=mesh,
        in_specs=(
            P("expert", "dp"),
            P("expert", "dp"),
            P("expert", None, "dp"),
            P("expert", "dp", None),
            P(),
            P("expert", None),
        ),
        out_specs=(
            P("expert", None, "dp"),
            P("expert", "dp", None),
            P("expert", "dp"),
            P("expert", None),
        ),
        check_vma=False,
    )
```

```python
import jax
import jax.numpy as jnp
from jax import lax
from jax.experimental import pallas as pl
from jax.experimental.pallas import tpu as pltpu
from jax.sharding import PartitionSpec as P

GELU_SCALE = 0.7978845608
CUBIC_COEF = 0.044715

NY, NZ = 8, 4
MIB = 1024 * 1024
BF, F32 = jnp.bfloat16, jnp.float32


def dp_index(y, z, core):
    return (y * NZ + z) * 2 + core


INNER = [[dp_index(y, z, 0) for y in range(NY)] for z in range(NZ)] + [
    [dp_index(2 * q + p, z, 1) for p in range(2) for z in range(NZ)] for q in range(4)
]
OUTER = [[dp_index(y, z, 0) for z in range(NZ)] for y in range(NY)] + [
    [dp_index(2 * q + p, z, 1) for q in range(4)] for p in range(2) for z in range(NZ)
]
SWAP = [(d, d ^ 1) for d in range(NY * NZ * 2)]


def gelu_parts(preact):
    inner = GELU_SCALE * (preact + CUBIC_COEF * preact * preact * preact)
    tanh_part = jnp.tanh(inner)
    gelu_val = 0.5 * preact * (1.0 + tanh_part)
    gelu_slope = 0.5 * (1.0 + tanh_part) + 0.5 * preact * (
        1.0 - tanh_part * tanh_part
    ) * GELU_SCALE * (1.0 + 3.0 * CUBIC_COEF * preact * preact)
    return gelu_val, gelu_slope


def contract(left, right, left_axis, right_axis):
    return lax.dot_general(
        left, right, (((left_axis,), (right_axis,)), ((), ())), preferred_element_type=F32
    )


def onehot(base, chosen_row, tokens):
    rows = chosen_row.shape[1]
    ids = base + lax.broadcasted_iota(jnp.int32, (tokens, rows), 0)
    return jnp.where(ids == chosen_row, 1.0, 0.0).astype(BF)


def hi_lo(value):
    high = value.astype(BF)
    low = (value - high.astype(F32)).astype(BF)
    return high, low


def pick_kernel(
    base_ref, act_hbm, grad_hbm, chosen_hbm, out_ref, both_ref, chosen_ref, sems
):
    feats = act_hbm.shape[0]
    copies = [
        pltpu.make_async_copy(act_hbm, both_ref.at[pl.ds(0, feats)], sems.at[0]),
        pltpu.make_async_copy(grad_hbm, both_ref.at[pl.ds(feats, feats)], sems.at[1]),
        pltpu.make_async_copy(chosen_hbm, chosen_ref, sems.at[2]),
    ]
    for copy in copies:
        copy.start()
    for copy in copies:
        copy.wait()
    both = both_ref[...]
    for e in range(out_ref.shape[0]):
        sel = onehot(base_ref[0], chosen_ref[e : e + 1, :], both.shape[1])
        out_ref[e] = contract(both, sel, 1, 0).astype(BF)


def merge_kernel(parts_ref, out_ref):
    total = parts_ref[0].astype(F32)
    for k in range(1, parts_ref.shape[0]):
        total = total + parts_ref[k].astype(F32)
    total = total.astype(BF)
    for k in range(out_ref.shape[0]):
        out_ref[k] = total


def gate_tile(pairs):
    rows = [half.astype(F32) for pair in pairs for half in pair]
    rows.append(jnp.zeros((16 - len(rows), rows[0].shape[1]), F32))
    return jnp.concatenate(rows, axis=0).astype(BF)


def block_rows(slots_ref, slot, feats):
    return pl.ds(pl.multiple_of(slots_ref[slot] * feats, feats), feats)


def load_blocks(slots_ref, first, blocks_ref, x_ref, u_ref, x_sem, u_sem):
    outer, inner, both = blocks_ref.shape[:3]
    feats = both // 2
    for o in range(outer):
        for i in range(inner):
            at = block_rows(slots_ref, first + o * inner + i, feats)
            act, grad = (blocks_ref.at[o, i, pl.ds(h * feats, feats)] for h in range(2))
            pltpu.make_async_copy(act, x_ref.at[at], x_sem).start()
            pltpu.make_async_copy(grad, u_ref.at[at], u_sem).start()
    half = pl.ds(0, outer * inner * feats)
    return (
        pltpu.make_async_copy(x_ref.at[half], x_ref.at[half], x_sem),
        pltpu.make_async_copy(u_ref.at[half], u_ref.at[half], u_sem),
    )


def ready_kernel(slots_ref, own_ref, w_in_ref, x_ref, u_ref, turned_ref, x_sem, u_sem):
    arrived = load_blocks(slots_ref, 0, own_ref, x_ref, u_ref, x_sem, u_sem)
    turned_ref[...] = w_in_ref[...].T
    for copy in arrived:
        copy.wait()


def main_kernel(
    slots_ref, oth_ref, x_in, u_in, turned_ref, w_in_ref, w_out_ref, score_ref,
    x_ref, u_ref, back_ref, scaled_ref, gate_ref, send_ref, held_ref, x_sem, u_sem, w_sem,
):
    weights = pltpu.make_async_copy(w_out_ref, held_ref, w_sem)
    weights.start()
    slots = oth_ref.shape[0] * oth_ref.shape[1]
    feats = oth_ref.shape[2] // 2
    x_done, u_done = load_blocks(slots_ref, slots, oth_ref, x_ref, u_ref, x_sem, u_sem)
    x_done.wait()
    preact = contract(turned_ref[...], x_ref[...], 1, 0)
    u_done.wait()
    weights.wait()
    raw = contract(held_ref[...], u_ref[...], 1, 0)
    val, slope = gelu_parts(preact)
    hidden = val.astype(BF).astype(F32)
    score = score_ref[...]
    gate = jnp.sum(hidden * raw, axis=0, keepdims=True)
    back = (score * raw * slope).astype(BF)
    back_ref[...] = back
    scaled_ref[...] = (score * hidden).astype(BF)
    gate_ref[...] = gate
    for s in range(slots):
        at = block_rows(slots_ref, slots + s, feats)
        send_ref[pl.ds(s * feats, feats), :] = contract(w_in_ref[at, :], back, 1, 0).astype(BF)
    send_ref[pl.ds(slots * feats, 16), :] = gate_tile([hi_lo(gate)])


def weight_kernel(x_ref, u_ref, back_ref, scaled_ref, gin_ref, gout_ref):
    gin_ref[...] = contract(x_ref[...], back_ref[...], 1, 1).astype(BF)
    gout_ref[...] = contract(scaled_ref[...], u_ref[...], 1, 1).astype(BF)


def pair_kernel(slots_ref, w_in_ref, back_ref, gate_ref, got_ref, out_ref):
    parts, rows = out_ref.shape[0], out_ref.shape[1] - 16
    feats = rows // 8
    back = back_ref[...]
    tile = got_ref[pl.ds(parts * rows, 16), :].astype(F32)
    high, low = hi_lo(gate_ref[...])
    gate = (high.astype(F32) + low.astype(F32)) + (tile[0:1] + tile[1:2])
    packed = gate_tile([hi_lo(gate)])
    for k in range(parts):
        for i in range(8):
            s = k * 8 + i
            mine = contract(w_in_ref[block_rows(slots_ref, s, feats), :], back, 1, 0)
            other = got_ref[pl.ds(s * feats, feats), :].astype(F32)
            out_ref[k, pl.ds(i * feats, feats), :] = (mine + other).astype(BF)
        out_ref[k, rows:, :] = packed


def outer_kernel(got_ref, out_ref):
    count, rows = out_ref.shape[0], out_ref.shape[1] - 16
    base = count * rows
    tiles = [got_ref[o, pl.ds(base, 16), :].astype(F32) for o in range(4)]
    packed = gate_tile([(t[0:1], t[1:2]) for t in tiles])
    for i in range(count):
        at = pl.ds(i * rows, rows)
        total = got_ref[0, at, :].astype(F32)
        for o in range(1, 4):
            total = total + got_ref[o, at, :].astype(F32)
        out_ref[i, :rows, :] = total.astype(BF)
        out_ref[i, rows:, :] = packed


def inner_kernel(core_ref, got_ref, out_ref, gate_ref):
    rows = out_ref.shape[1]
    sources = got_ref.shape[0]
    total = got_ref[0, :rows, :].astype(F32)
    for i in range(1, sources):
        total = total + got_ref[i, :rows, :].astype(F32)
    total = total.astype(BF)
    for k in range(out_ref.shape[0]):
        out_ref[k] = total
    tiles = [got_ref[i, rows:, :].astype(F32) for i in range(sources)]
    gates = [[t[2 * o : 2 * o + 1] + t[2 * o + 1 : 2 * o + 2] for o in range(4)] for t in tiles]
    first = core_ref[0] == 0
    gate = jnp.zeros((1, got_ref.shape[2]), F32)
    for y in range(NY):
        for z in range(NZ):
            gate = gate + jnp.where(first, gates[y][z], gates[(y % 2) * NZ + z][y // 2])
    gate_ref[...] = gate


def scatter_kernel(base_ref, terms_ref, chosen_ref, out_ref):
    tokens = out_ref.shape[1]
    total = jnp.zeros(out_ref.shape, F32)
    for e in range(terms_ref.shape[0]):
        sel = onehot(base_ref[0], chosen_ref[e : e + 1, :], tokens)
        total = total + contract(terms_ref[e], sel, 1, 1)
    out_ref[...] = total.astype(BF)


SMEM = pl.BlockSpec(memory_space=pltpu.SMEM)
VMEM = pl.BlockSpec(memory_space=pltpu.VMEM)
HBM = pl.BlockSpec(memory_space=pltpu.HBM)
ANY = pl.BlockSpec(memory_space=pl.ANY)


def call(kernel, specs, outs, *args, scratch=(), alias=None, mib=16, flops=0, moved=0):
    shapes = [jax.ShapeDtypeStruct(s, t) for s, t in outs]
    single = len(shapes) == 1
    return pl.pallas_call(
        kernel,
        out_shape=shapes[0] if single else shapes,
        in_specs=specs,
        out_specs=VMEM if single else [VMEM] * len(shapes),
        scratch_shapes=scratch,
        input_output_aliases=alias or {},
        cost_estimate=pl.CostEstimate(flops=flops, bytes_accessed=moved, transcendentals=0),
        compiler_params=pltpu.CompilerParams(vmem_limit_bytes=mib * MIB),
    )(*args)


def in_hbm(value):
    return pltpu.with_memory_space_constraint(value, pltpu.HBM)


def exchange(parts, axis, groups=None):
    return lax.all_to_all(parts, axis, 0, 0, axis_index_groups=groups)


def block_table(core):
    o = jnp.arange(4, dtype=jnp.int32)[:, None]
    i = jnp.arange(8, dtype=jnp.int32)[None, :]
    zero = dp_index(i, o, 0)
    one = dp_index(2 * o + i // NZ, i % NZ, 1)
    return jnp.where(core == 0, zero, one).reshape(-1)


def per_device(activations, out_grad, w_in, w_out, chosen, gate_scores):
    tokens, feats = activations.shape
    experts, rows = chosen.shape
    depth, units = w_in.shape[1], w_in.shape[2]
    base = (lax.axis_index("expert") * tokens).astype(jnp.int32).reshape(1)
    core = lax.axis_index("dp").astype(jnp.int32) & 1
    slots = jnp.concatenate([block_table(core), block_table(1 - core)])
    count = slots.shape[0] // 2

    picked = call(
        pick_kernel,
        [SMEM, HBM, HBM, HBM],
        [((experts, 2 * feats, rows), BF)],
        base, in_hbm(activations.T), in_hbm(out_grad.T), in_hbm(chosen),
        scratch=[
            pltpu.VMEM((2 * feats, tokens), BF),
            pltpu.VMEM((experts, rows), jnp.int32),
            pltpu.SemaphoreType.DMA((3,)),
        ],
    )
    picked = exchange(picked, "expert")
    mine = call(merge_kernel, [VMEM], [((8, 2 * feats, rows), BF)], picked)
    inner = exchange(mine, "dp", INNER)
    own = exchange(jnp.broadcast_to(inner[None], (4,) + inner.shape), "dp", OUTER)
    other = lax.ppermute(own, "dp", SWAP)
    sems = [pltpu.SemaphoreType.DMA] * 2
    held = [((depth, rows), BF), ((depth, rows), BF)]
    x, u, turned = call(
        ready_kernel, [SMEM, ANY, VMEM], held + [((units, depth), BF)], slots, own, w_in[0],
        scratch=sems, flops=2 * MIB, moved=6 * MIB,
    )
    x, u, back, scaled, gate, send = call(
        main_kernel,
        [SMEM, ANY] + [VMEM] * 4 + [HBM, VMEM],
        held
        + [
            ((units, rows), BF),
            ((units, rows), BF),
            ((1, rows), F32),
            ((count * feats + 16, rows), BF),
        ],
        slots, other, x, u, turned, w_in[0], in_hbm(w_out[0]), gate_scores,
        scratch=[pltpu.VMEM((units, depth), BF)] + [pltpu.SemaphoreType.DMA] * 3, alias={2: 0, 3: 1},
    )
    got = lax.ppermute(send, "dp", SWAP)
    weight_grads = call(
        weight_kernel,
        [VMEM] * 4,
        [((depth, units), BF), ((units, depth), BF)],
        x, u, back, scaled, flops=4 * depth * units * rows, moved=6 * depth * rows,
    )
    got, weight_in_grad, weight_out_grad = lax.optimization_barrier((got, *weight_grads))
    part = call(
        pair_kernel,
        [SMEM] + [VMEM] * 4,
        [((4, 8 * feats + 16, rows), BF)],
        slots, w_in[0], back, gate, got,
    )
    part = exchange(part, "dp", OUTER)
    part = call(outer_kernel, [VMEM], [((8, feats + 16, rows), BF)], part)
    part = exchange(part, "dp", INNER)
    term, gate_grad = call(
        inner_kernel, [SMEM, VMEM], [((experts, feats, rows), BF), ((1, rows), F32)],
        core.reshape(1), part,
    )
    terms = exchange(term, "expert")
    act_grad = call(
        scatter_kernel, [SMEM, VMEM, VMEM], [((feats, tokens), BF)], base, terms, chosen
    )
    return weight_in_grad[None], weight_out_grad[None], act_grad.T, gate_grad


def solution(mesh):
    return jax.shard_map(
        per_device,
        mesh=mesh,
        in_specs=(
            P("expert", "dp"),
            P("expert", "dp"),
            P("expert", None, "dp"),
            P("expert", "dp", None),
            P(),
            P("expert", None),
        ),
        out_specs=(
            P("expert", None, "dp"),
            P("expert", "dp", None),
            P("expert", "dp"),
            P("expert", None),
        ),
        check_vma=False,
    )
```

```python
import jax
import jax.numpy as jnp
from jax import lax
from jax.experimental import pallas as pl
from jax.experimental.pallas import tpu as pltpu
from jax.sharding import PartitionSpec as P

GELU_SCALE = 0.7978845608
CUBIC_COEF = 0.044715

NY, NZ = 8, 4
MIB = 1024 * 1024
BF, F32 = jnp.bfloat16, jnp.float32


def dp_index(y, z, core):
    return (y * NZ + z) * 2 + core


INNER = [[dp_index(y, z, 0) for y in range(NY)] for z in range(NZ)] + [
    [dp_index(2 * q + p, z, 1) for p in range(2) for z in range(NZ)] for q in range(4)
]
OUTER = [[dp_index(y, z, 0) for z in range(NZ)] for y in range(NY)] + [
    [dp_index(2 * q + p, z, 1) for q in range(4)] for p in range(2) for z in range(NZ)
]
EVERY_OTHER_Y = [
    [[dp_index(2 * q + p, z, c) for q in range(4)] for p in range(2) for z in range(NZ)]
    for c in range(2)
]
ALL_Z = [[[dp_index(y, z, c) for z in range(NZ)] for y in range(NY)] for c in range(2)]
FIRST = EVERY_OTHER_Y[0] + ALL_Z[1]
SECOND = ALL_Z[0] + EVERY_OTHER_Y[1]
NEIGHBOUR = [
    (dp_index(y, z, c), dp_index((y + (1 if y % 2 == c else NY - 1)) % NY, z, c))
    for y in range(NY)
    for z in range(NZ)
    for c in range(2)
]
SWAP = [(d, d ^ 1) for d in range(NY * NZ * 2)]


def gelu_parts(preact):
    inner = GELU_SCALE * (preact + CUBIC_COEF * preact * preact * preact)
    tanh_part = jnp.tanh(inner)
    gelu_val = 0.5 * preact * (1.0 + tanh_part)
    gelu_slope = 0.5 * (1.0 + tanh_part) + 0.5 * preact * (
        1.0 - tanh_part * tanh_part
    ) * GELU_SCALE * (1.0 + 3.0 * CUBIC_COEF * preact * preact)
    return gelu_val, gelu_slope


def contract(left, right, left_axis, right_axis):
    return lax.dot_general(
        left, right, (((left_axis,), (right_axis,)), ((), ())), preferred_element_type=F32
    )


def onehot(base, chosen_row, tokens):
    rows = chosen_row.shape[1]
    ids = base + lax.broadcasted_iota(jnp.int32, (tokens, rows), 0)
    return jnp.where(ids == chosen_row, 1.0, 0.0).astype(BF)


def hi_lo(value):
    high = value.astype(BF)
    low = (value - high.astype(F32)).astype(BF)
    return high, low


def pick_kernel(
    base_ref, act_hbm, grad_hbm, chosen_hbm, out_ref, both_ref, chosen_ref, sems
):
    feats = act_hbm.shape[0]
    copies = [
        pltpu.make_async_copy(act_hbm, both_ref.at[pl.ds(0, feats)], sems.at[0]),
        pltpu.make_async_copy(grad_hbm, both_ref.at[pl.ds(feats, feats)], sems.at[1]),
        pltpu.make_async_copy(chosen_hbm, chosen_ref, sems.at[2]),
    ]
    for copy in copies:
        copy.start()
    for copy in copies:
        copy.wait()
    both = both_ref[...]
    for e in range(out_ref.shape[0]):
        sel = onehot(base_ref[0], chosen_ref[e : e + 1, :], both.shape[1])
        out_ref[e] = contract(both, sel, 1, 0).astype(BF)


def merge_kernel(parts_ref, out_ref):
    total = parts_ref[0].astype(F32)
    for k in range(1, parts_ref.shape[0]):
        total = total + parts_ref[k].astype(F32)
    total = total.astype(BF)
    for k in range(out_ref.shape[0]):
        out_ref[k] = total


def gate_tile(pairs):
    rows = [half.astype(F32) for pair in pairs for half in pair]
    rows.append(jnp.zeros((16 - len(rows), rows[0].shape[1]), F32))
    return jnp.concatenate(rows, axis=0).astype(BF)


def block_rows(slots_ref, slot, feats):
    return pl.ds(pl.multiple_of(slots_ref[slot] * feats, feats), feats)


def load_blocks(slots_ref, first, blocks_ref, x_ref, u_ref, x_sem, u_sem):
    outer, inner, both = blocks_ref.shape[:3]
    feats = both // 2
    for o in range(outer):
        for i in range(inner):
            at = block_rows(slots_ref, first + o * inner + i, feats)
            act, grad = (blocks_ref.at[o, i, pl.ds(h * feats, feats)] for h in range(2))
            pltpu.make_async_copy(act, x_ref.at[at], x_sem).start()
            pltpu.make_async_copy(grad, u_ref.at[at], u_sem).start()
    half = pl.ds(0, outer * inner * feats)
    return (
        pltpu.make_async_copy(x_ref.at[half], x_ref.at[half], x_sem),
        pltpu.make_async_copy(u_ref.at[half], u_ref.at[half], u_sem),
    )


def ready_kernel(
    slots_ref, own_ref, oth_ref, w_in_ref, x_ref, u_ref, turned_ref, x_sem, u_sem
):
    count = own_ref.shape[0] * own_ref.shape[1]
    arrived = load_blocks(slots_ref, 0, own_ref, x_ref, u_ref, x_sem.at[0], u_sem.at[0])
    arrived += load_blocks(slots_ref, count, oth_ref, x_ref, u_ref, x_sem.at[1], u_sem.at[1])
    turned_ref[...] = w_in_ref[...].T
    for copy in arrived:
        copy.wait()


def more_kernel(slots_ref, pair_ref, x_in, u_in, x_ref, u_ref, x_sem, u_sem):
    count = pair_ref.shape[0] * pair_ref.shape[1]
    for copy in load_blocks(slots_ref, 2 * count, pair_ref, x_ref, u_ref, x_sem, u_sem):
        copy.wait()


def main_kernel(
    slots_ref, oth_ref, x_in, u_in, turned_ref, w_in_ref, w_out_ref, score_ref,
    x_ref, u_ref, back_ref, scaled_ref, gate_ref, send_ref, held_ref, x_sem, u_sem, w_sem,
):
    weights = pltpu.make_async_copy(w_out_ref, held_ref, w_sem)
    weights.start()
    count = oth_ref.shape[0] * oth_ref.shape[1]
    feats = oth_ref.shape[2] // 2
    x_done, u_done = load_blocks(slots_ref, 3 * count, oth_ref, x_ref, u_ref, x_sem, u_sem)
    x_done.wait()
    preact = contract(turned_ref[...], x_ref[...], 1, 0)
    u_done.wait()
    weights.wait()
    raw = contract(held_ref[...], u_ref[...], 1, 0)
    val, slope = gelu_parts(preact)
    hidden = val.astype(BF).astype(F32)
    score = score_ref[...]
    gate = jnp.sum(hidden * raw, axis=0, keepdims=True)
    back = (score * raw * slope).astype(BF)
    back_ref[...] = back
    scaled_ref[...] = (score * hidden).astype(BF)
    gate_ref[...] = gate
    slots = 2 * count
    for s in range(slots):
        at = block_rows(slots_ref, 3 * slots + s, feats)
        send_ref[pl.ds(s * feats, feats), :] = contract(w_in_ref[at, :], back, 1, 0).astype(BF)
    send_ref[pl.ds(slots * feats, 16), :] = gate_tile([hi_lo(gate)])


def weight_kernel(x_ref, u_ref, back_ref, scaled_ref, gin_ref, gout_ref):
    gin_ref[...] = contract(x_ref[...], back_ref[...], 1, 1).astype(BF)
    gout_ref[...] = contract(scaled_ref[...], u_ref[...], 1, 1).astype(BF)


def pair_kernel(slots_ref, w_in_ref, back_ref, gate_ref, got_ref, out_ref):
    parts, rows = out_ref.shape[0], out_ref.shape[1] - 16
    feats = rows // 8
    back = back_ref[...]
    tile = got_ref[pl.ds(parts * rows, 16), :].astype(F32)
    high, low = hi_lo(gate_ref[...])
    gate = (high.astype(F32) + low.astype(F32)) + (tile[0:1] + tile[1:2])
    packed = gate_tile([hi_lo(gate)])
    for k in range(parts):
        for i in range(8):
            s = k * 8 + i
            mine = contract(w_in_ref[block_rows(slots_ref, 2 * 8 * parts + s, feats), :], back, 1, 0)
            other = got_ref[pl.ds(s * feats, feats), :].astype(F32)
            out_ref[k, pl.ds(i * feats, feats), :] = (mine + other).astype(BF)
        out_ref[k, rows:, :] = packed


def outer_kernel(got_ref, out_ref):
    count, rows = out_ref.shape[0], out_ref.shape[1] - 16
    base = count * rows
    tiles = [got_ref[o, pl.ds(base, 16), :].astype(F32) for o in range(4)]
    packed = gate_tile([(t[0:1], t[1:2]) for t in tiles])
    for i in range(count):
        at = pl.ds(i * rows, rows)
        total = got_ref[0, at, :].astype(F32)
        for o in range(1, 4):
            total = total + got_ref[o, at, :].astype(F32)
        out_ref[i, :rows, :] = total.astype(BF)
        out_ref[i, rows:, :] = packed


def inner_kernel(core_ref, got_ref, out_ref, gate_ref):
    rows = out_ref.shape[1]
    sources = got_ref.shape[0]
    total = got_ref[0, :rows, :].astype(F32)
    for i in range(1, sources):
        total = total + got_ref[i, :rows, :].astype(F32)
    total = total.astype(BF)
    for k in range(out_ref.shape[0]):
        out_ref[k] = total
    tiles = [got_ref[i, rows:, :].astype(F32) for i in range(sources)]
    gates = [[t[2 * o : 2 * o + 1] + t[2 * o + 1 : 2 * o + 2] for o in range(4)] for t in tiles]
    first = core_ref[0] == 0
    gate = jnp.zeros((1, got_ref.shape[2]), F32)
    for y in range(NY):
        for z in range(NZ):
            gate = gate + jnp.where(first, gates[y][z], gates[(y % 2) * NZ + z][y // 2])
    gate_ref[...] = gate


def scatter_kernel(base_ref, terms_ref, chosen_ref, out_ref):
    tokens = out_ref.shape[1]
    total = jnp.zeros(out_ref.shape, F32)
    for e in range(terms_ref.shape[0]):
        sel = onehot(base_ref[0], chosen_ref[e : e + 1, :], tokens)
        total = total + contract(terms_ref[e], sel, 1, 1)
    out_ref[...] = total.astype(BF)


SMEM = pl.BlockSpec(memory_space=pltpu.SMEM)
VMEM = pl.BlockSpec(memory_space=pltpu.VMEM)
HBM = pl.BlockSpec(memory_space=pltpu.HBM)
ANY = pl.BlockSpec(memory_space=pl.ANY)


def call(kernel, specs, outs, *args, scratch=(), alias=None, mib=16, flops=0, moved=0):
    shapes = [jax.ShapeDtypeStruct(s, t) for s, t in outs]
    single = len(shapes) == 1
    return pl.pallas_call(
        kernel,
        out_shape=shapes[0] if single else shapes,
        in_specs=specs,
        out_specs=VMEM if single else [VMEM] * len(shapes),
        scratch_shapes=scratch,
        input_output_aliases=alias or {},
        cost_estimate=pl.CostEstimate(flops=flops, bytes_accessed=moved, transcendentals=0),
        compiler_params=pltpu.CompilerParams(vmem_limit_bytes=mib * MIB),
    )(*args)


def in_hbm(value):
    return pltpu.with_memory_space_constraint(value, pltpu.HBM)


def exchange(parts, axis, groups=None):
    return lax.all_to_all(parts, axis, 0, 0, axis_index_groups=groups)


def block_table(core):
    o = jnp.arange(4, dtype=jnp.int32)[:, None]
    i = jnp.arange(8, dtype=jnp.int32)[None, :]
    zero = dp_index(i, o, 0)
    one = dp_index(2 * o + i // NZ, i % NZ, 1)
    return jnp.where(core == 0, zero, one).reshape(-1)


def half_table(core, parity):
    o = jnp.arange(4, dtype=jnp.int32)[:, None]
    i = jnp.arange(4, dtype=jnp.int32)[None, :]
    zero = dp_index(2 * i + parity, o, 0)
    one = dp_index(2 * o + parity, i, 1)
    return jnp.where(core == 0, zero, one).reshape(-1)


def per_device(activations, out_grad, w_in, w_out, chosen, gate_scores):
    tokens, feats = activations.shape
    experts, rows = chosen.shape
    depth, units = w_in.shape[1], w_in.shape[2]
    base = (lax.axis_index("expert") * tokens).astype(jnp.int32).reshape(1)
    index = lax.axis_index("dp").astype(jnp.int32)
    core, parity = index & 1, (index >> 3) & 1
    slots = jnp.concatenate(
        [
            half_table(core, parity),
            half_table(1 - core, parity),
            half_table(core, 1 - parity),
            half_table(1 - core, 1 - parity),
            block_table(core),
            block_table(1 - core),
        ]
    )
    count = slots.shape[0] // 4

    picked = call(
        pick_kernel,
        [SMEM, HBM, HBM, HBM],
        [((experts, 2 * feats, rows), BF)],
        base, in_hbm(activations.T), in_hbm(out_grad.T), in_hbm(chosen),
        scratch=[
            pltpu.VMEM((2 * feats, tokens), BF),
            pltpu.VMEM((experts, rows), jnp.int32),
            pltpu.SemaphoreType.DMA((3,)),
        ],
    )
    picked = exchange(picked, "expert")
    mine = call(merge_kernel, [VMEM], [((4, 2 * feats, rows), BF)], picked)
    first = exchange(mine, "dp", FIRST)
    own = exchange(jnp.broadcast_to(first[None], (4,) + first.shape), "dp", SECOND)
    pair = lax.ppermute(own, "dp", NEIGHBOUR)
    other = lax.ppermute(own, "dp", SWAP)
    sems = [pltpu.SemaphoreType.DMA] * 2
    held = [((depth, rows), BF), ((depth, rows), BF)]
    x, u, turned = call(
        ready_kernel, [SMEM, ANY, ANY, VMEM], held + [((units, depth), BF)],
        slots, own, other, w_in[0],
        scratch=[pltpu.SemaphoreType.DMA((2,))] * 2, flops=2 * MIB, moved=6 * MIB,
    )
    pair, x, u, turned = lax.optimization_barrier((pair, x, u, turned))
    other = lax.ppermute(pair, "dp", SWAP)
    x, u = call(
        more_kernel, [SMEM, ANY, VMEM, VMEM], held, slots, pair, x, u,
        scratch=sems, alias={2: 0, 3: 1}, flops=2 * MIB, moved=3 * MIB,
    )
    x, u, back, scaled, gate, send = call(
        main_kernel,
        [SMEM, ANY] + [VMEM] * 4 + [HBM, VMEM],
        held
        + [
            ((units, rows), BF),
            ((units, rows), BF),
            ((1, rows), F32),
            ((count * feats + 16, rows), BF),
        ],
        slots, other, x, u, turned, w_in[0], in_hbm(w_out[0]), gate_scores,
        scratch=[pltpu.VMEM((units, depth), BF)] + [pltpu.SemaphoreType.DMA] * 3, alias={2: 0, 3: 1},
    )
    got = lax.ppermute(send, "dp", SWAP)
    weight_grads = call(
        weight_kernel,
        [VMEM] * 4,
        [((depth, units), BF), ((units, depth), BF)],
        x, u, back, scaled, flops=4 * depth * units * rows, moved=6 * depth * rows,
    )
    got, weight_in_grad, weight_out_grad = lax.optimization_barrier((got, *weight_grads))
    part = call(
        pair_kernel,
        [SMEM] + [VMEM] * 4,
        [((4, 8 * feats + 16, rows), BF)],
        slots, w_in[0], back, gate, got,
    )
    part = exchange(part, "dp", OUTER)
    part = call(outer_kernel, [VMEM], [((8, feats + 16, rows), BF)], part)
    part = exchange(part, "dp", INNER)
    term, gate_grad = call(
        inner_kernel, [SMEM, VMEM], [((experts, feats, rows), BF), ((1, rows), F32)],
        core.reshape(1), part,
    )
    terms = exchange(term, "expert")
    act_grad = call(
        scatter_kernel, [SMEM, VMEM, VMEM], [((feats, tokens), BF)], base, terms, chosen
    )
    return weight_in_grad[None], weight_out_grad[None], act_grad.T, gate_grad


def solution(mesh):
    return jax.shard_map(
        per_device,
        mesh=mesh,
        in_specs=(
            P("expert", "dp"),
            P("expert", "dp"),
            P("expert", None, "dp"),
            P("expert", "dp", None),
            P(),
            P("expert", None),
        ),
        out_specs=(
            P("expert", None, "dp"),
            P("expert", "dp", None),
            P("expert", "dp"),
            P("expert", None),
        ),
        check_vma=False,
    )
```

```python
import jax
import jax.numpy as jnp
from jax import lax
from jax.experimental import pallas as pl
from jax.experimental.pallas import tpu as pltpu
from jax.sharding import PartitionSpec as P

GELU_SCALE = 0.7978845608
CUBIC_COEF = 0.044715

NY, NZ = 8, 4
MIB = 1024 * 1024
BF, F32 = jnp.bfloat16, jnp.float32


def dp_index(y, z, core):
    return (y * NZ + z) * 2 + core


INNER = [[dp_index(y, z, 1) for y in range(NY)] for z in range(NZ)] + [
    [dp_index(2 * q + p, z, 0) for p in range(2) for z in range(NZ)] for q in range(4)
]
OUTER = [[dp_index(y, z, 1) for z in range(NZ)] for y in range(NY)] + [
    [dp_index(2 * q + p, z, 0) for q in range(4)] for p in range(2) for z in range(NZ)
]
SWAP = [(d, d ^ 1) for d in range(NY * NZ * 2)]


def gelu_parts(preact):
    inner = GELU_SCALE * (preact + CUBIC_COEF * preact * preact * preact)
    tanh_part = jnp.tanh(inner)
    gelu_val = 0.5 * preact * (1.0 + tanh_part)
    gelu_slope = 0.5 * (1.0 + tanh_part) + 0.5 * preact * (
        1.0 - tanh_part * tanh_part
    ) * GELU_SCALE * (1.0 + 3.0 * CUBIC_COEF * preact * preact)
    return gelu_val, gelu_slope


def contract(left, right, left_axis, right_axis):
    return lax.dot_general(
        left, right, (((left_axis,), (right_axis,)), ((), ())), preferred_element_type=F32
    )


def onehot(base, chosen_row, tokens):
    rows = chosen_row.shape[1]
    ids = base + lax.broadcasted_iota(jnp.int32, (tokens, rows), 0)
    return jnp.where(ids == chosen_row, 1.0, 0.0).astype(BF)


def hi_lo(value):
    high = value.astype(BF)
    low = (value - high.astype(F32)).astype(BF)
    return high, low


def pick_kernel(
    base_ref, act_hbm, grad_hbm, chosen_hbm, out_ref, both_ref, chosen_ref, sems
):
    feats = act_hbm.shape[0]
    copies = [
        pltpu.make_async_copy(act_hbm, both_ref.at[pl.ds(0, feats)], sems.at[0]),
        pltpu.make_async_copy(grad_hbm, both_ref.at[pl.ds(feats, feats)], sems.at[1]),
        pltpu.make_async_copy(chosen_hbm, chosen_ref, sems.at[2]),
    ]
    for copy in copies:
        copy.start()
    for copy in copies:
        copy.wait()
    both = both_ref[...]
    for e in range(out_ref.shape[0]):
        sel = onehot(base_ref[0], chosen_ref[e : e + 1, :], both.shape[1])
        out_ref[e] = contract(both, sel, 1, 0).astype(BF)


def merge_kernel(parts_ref, out_ref):
    total = parts_ref[0].astype(F32)
    for k in range(1, parts_ref.shape[0]):
        total = total + parts_ref[k].astype(F32)
    total = total.astype(BF)
    for k in range(out_ref.shape[0]):
        out_ref[k] = total


def gate_tile(pairs):
    rows = [half.astype(F32) for pair in pairs for half in pair]
    rows.append(jnp.zeros((16 - len(rows), rows[0].shape[1]), F32))
    return jnp.concatenate(rows, axis=0).astype(BF)


def block_rows(slots_ref, slot, feats):
    return pl.ds(pl.multiple_of(slots_ref[slot] * feats, feats), feats)


def load_blocks(slots_ref, first, blocks_ref, x_ref, u_ref, x_sem, u_sem):
    outer, inner, both = blocks_ref.shape[:3]
    feats = both // 2
    for o in range(outer):
        for i in range(inner):
            at = block_rows(slots_ref, first + o * inner + i, feats)
            act, grad = (blocks_ref.at[o, i, pl.ds(h * feats, feats)] for h in range(2))
            pltpu.make_async_copy(act, x_ref.at[at], x_sem).start()
            pltpu.make_async_copy(grad, u_ref.at[at], u_sem).start()
    half = pl.ds(0, outer * inner * feats)
    return (
        pltpu.make_async_copy(x_ref.at[half], x_ref.at[half], x_sem),
        pltpu.make_async_copy(u_ref.at[half], u_ref.at[half], u_sem),
    )


def ready_kernel(slots_ref, own_ref, w_in_ref, x_ref, u_ref, turned_ref, x_sem, u_sem):
    arrived = load_blocks(slots_ref, 0, own_ref, x_ref, u_ref, x_sem, u_sem)
    turned_ref[...] = w_in_ref[...].T
    for copy in arrived:
        copy.wait()


def main_kernel(
    slots_ref, oth_ref, x_in, u_in, turned_ref, w_in_ref, w_out_ref, score_ref,
    x_ref, u_ref, back_ref, scaled_ref, gate_ref, send_ref, held_ref, x_sem, u_sem, w_sem,
):
    weights = pltpu.make_async_copy(w_out_ref, held_ref, w_sem)
    weights.start()
    slots = oth_ref.shape[0] * oth_ref.shape[1]
    feats = oth_ref.shape[2] // 2
    x_done, u_done = load_blocks(slots_ref, slots, oth_ref, x_ref, u_ref, x_sem, u_sem)
    x_done.wait()
    preact = contract(turned_ref[...], x_ref[...], 1, 0)
    u_done.wait()
    weights.wait()
    raw = contract(held_ref[...], u_ref[...], 1, 0)
    val, slope = gelu_parts(preact)
    hidden = val.astype(BF).astype(F32)
    score = score_ref[...]
    gate = jnp.sum(hidden * raw, axis=0, keepdims=True)
    back = (score * raw * slope).astype(BF)
    back_ref[...] = back
    scaled_ref[...] = (score * hidden).astype(BF)
    gate_ref[...] = gate
    for s in range(slots):
        at = block_rows(slots_ref, slots + s, feats)
        send_ref[pl.ds(s * feats, feats), :] = contract(w_in_ref[at, :], back, 1, 0).astype(BF)
    send_ref[pl.ds(slots * feats, 16), :] = gate_tile([hi_lo(gate)])


def weight_kernel(x_ref, u_ref, back_ref, scaled_ref, gin_ref, gout_ref):
    gin_ref[...] = contract(x_ref[...], back_ref[...], 1, 1).astype(BF)
    gout_ref[...] = contract(scaled_ref[...], u_ref[...], 1, 1).astype(BF)


def pair_kernel(slots_ref, w_in_ref, back_ref, gate_ref, got_ref, out_ref):
    parts, rows = out_ref.shape[0], out_ref.shape[1] - 16
    feats = rows // 8
    back = back_ref[...]
    tile = got_ref[pl.ds(parts * rows, 16), :].astype(F32)
    high, low = hi_lo(gate_ref[...])
    gate = (high.astype(F32) + low.astype(F32)) + (tile[0:1] + tile[1:2])
    packed = gate_tile([hi_lo(gate)])
    for k in range(parts):
        for i in range(8):
            s = k * 8 + i
            mine = contract(w_in_ref[block_rows(slots_ref, s, feats), :], back, 1, 0)
            other = got_ref[pl.ds(s * feats, feats), :].astype(F32)
            out_ref[k, pl.ds(i * feats, feats), :] = (mine + other).astype(BF)
        out_ref[k, rows:, :] = packed


def outer_kernel(got_ref, out_ref):
    count, rows = out_ref.shape[0], out_ref.shape[1] - 16
    base = count * rows
    tiles = [got_ref[o, pl.ds(base, 16), :].astype(F32) for o in range(4)]
    packed = gate_tile([(t[0:1], t[1:2]) for t in tiles])
    for i in range(count):
        at = pl.ds(i * rows, rows)
        total = got_ref[0, at, :].astype(F32)
        for o in range(1, 4):
            total = total + got_ref[o, at, :].astype(F32)
        out_ref[i, :rows, :] = total.astype(BF)
        out_ref[i, rows:, :] = packed


def inner_kernel(core_ref, got_ref, out_ref, gate_ref):
    rows = out_ref.shape[1]
    sources = got_ref.shape[0]
    total = got_ref[0, :rows, :].astype(F32)
    for i in range(1, sources):
        total = total + got_ref[i, :rows, :].astype(F32)
    total = total.astype(BF)
    for k in range(out_ref.shape[0]):
        out_ref[k] = total
    tiles = [got_ref[i, rows:, :].astype(F32) for i in range(sources)]
    gates = [[t[2 * o : 2 * o + 1] + t[2 * o + 1 : 2 * o + 2] for o in range(4)] for t in tiles]
    along_y = core_ref[0] == 1
    gate = jnp.zeros((1, got_ref.shape[2]), F32)
    for y in range(NY):
        for z in range(NZ):
            gate = gate + jnp.where(along_y, gates[y][z], gates[(y % 2) * NZ + z][y // 2])
    gate_ref[...] = gate


def scatter_kernel(base_ref, terms_ref, chosen_ref, out_ref):
    tokens = out_ref.shape[1]
    total = jnp.zeros(out_ref.shape, F32)
    for e in range(terms_ref.shape[0]):
        sel = onehot(base_ref[0], chosen_ref[e : e + 1, :], tokens)
        total = total + contract(terms_ref[e], sel, 1, 1)
    out_ref[...] = total.astype(BF)


SMEM = pl.BlockSpec(memory_space=pltpu.SMEM)
VMEM = pl.BlockSpec(memory_space=pltpu.VMEM)
HBM = pl.BlockSpec(memory_space=pltpu.HBM)
ANY = pl.BlockSpec(memory_space=pl.ANY)


def call(kernel, specs, outs, *args, scratch=(), alias=None, mib=16, flops=0, moved=0):
    shapes = [jax.ShapeDtypeStruct(s, t) for s, t in outs]
    single = len(shapes) == 1
    return pl.pallas_call(
        kernel,
        out_shape=shapes[0] if single else shapes,
        in_specs=specs,
        out_specs=VMEM if single else [VMEM] * len(shapes),
        scratch_shapes=scratch,
        input_output_aliases=alias or {},
        cost_estimate=pl.CostEstimate(flops=flops, bytes_accessed=moved, transcendentals=0),
        compiler_params=pltpu.CompilerParams(vmem_limit_bytes=mib * MIB),
    )(*args)


def in_hbm(value):
    return pltpu.with_memory_space_constraint(value, pltpu.HBM)


def exchange(parts, axis, groups=None):
    return lax.all_to_all(parts, axis, 0, 0, axis_index_groups=groups)


def block_table(core):
    o = jnp.arange(4, dtype=jnp.int32)[:, None]
    i = jnp.arange(8, dtype=jnp.int32)[None, :]
    zero = dp_index(2 * o + i // NZ, i % NZ, 0)
    one = dp_index(i, o, 1)
    return jnp.where(core == 0, zero, one).reshape(-1)


def per_device(activations, out_grad, w_in, w_out, chosen, gate_scores):
    tokens, feats = activations.shape
    experts, rows = chosen.shape
    depth, units = w_in.shape[1], w_in.shape[2]
    base = (lax.axis_index("expert") * tokens).astype(jnp.int32).reshape(1)
    core = lax.axis_index("dp").astype(jnp.int32) & 1
    slots = jnp.concatenate([block_table(core), block_table(1 - core)])
    count = slots.shape[0] // 2

    picked = call(
        pick_kernel,
        [SMEM, HBM, HBM, HBM],
        [((experts, 2 * feats, rows), BF)],
        base, in_hbm(activations.T), in_hbm(out_grad.T), in_hbm(chosen),
        scratch=[
            pltpu.VMEM((2 * feats, tokens), BF),
            pltpu.VMEM((experts, rows), jnp.int32),
            pltpu.SemaphoreType.DMA((3,)),
        ],
    )
    picked = exchange(picked, "expert")
    mine = call(merge_kernel, [VMEM], [((8, 2 * feats, rows), BF)], picked)
    inner = exchange(mine, "dp", INNER)
    own = exchange(jnp.broadcast_to(inner[None], (4,) + inner.shape), "dp", OUTER)
    other = lax.ppermute(own, "dp", SWAP)
    sems = [pltpu.SemaphoreType.DMA] * 2
    held = [((depth, rows), BF), ((depth, rows), BF)]
    x, u, turned = call(
        ready_kernel, [SMEM, ANY, VMEM], held + [((units, depth), BF)], slots, own, w_in[0],
        scratch=sems, flops=2 * MIB, moved=6 * MIB,
    )
    x, u, back, scaled, gate, send = call(
        main_kernel,
        [SMEM, ANY] + [VMEM] * 4 + [HBM, VMEM],
        held
        + [
            ((units, rows), BF),
            ((units, rows), BF),
            ((1, rows), F32),
            ((count * feats + 16, rows), BF),
        ],
        slots, other, x, u, turned, w_in[0], in_hbm(w_out[0]), gate_scores,
        scratch=[pltpu.VMEM((units, depth), BF)] + [pltpu.SemaphoreType.DMA] * 3, alias={2: 0, 3: 1},
    )
    got = lax.ppermute(send, "dp", SWAP)
    weight_grads = call(
        weight_kernel,
        [VMEM] * 4,
        [((depth, units), BF), ((units, depth), BF)],
        x, u, back, scaled, flops=4 * depth * units * rows, moved=6 * depth * rows,
    )
    got, weight_in_grad, weight_out_grad = lax.optimization_barrier((got, *weight_grads))
    part = call(
        pair_kernel,
        [SMEM] + [VMEM] * 4,
        [((4, 8 * feats + 16, rows), BF)],
        slots, w_in[0], back, gate, got,
    )
    part = exchange(part, "dp", OUTER)
    part = call(outer_kernel, [VMEM], [((8, feats + 16, rows), BF)], part)
    part = exchange(part, "dp", INNER)
    term, gate_grad = call(
        inner_kernel, [SMEM, VMEM], [((experts, feats, rows), BF), ((1, rows), F32)],
        core.reshape(1), part,
    )
    terms = exchange(term, "expert")
    act_grad = call(
        scatter_kernel, [SMEM, VMEM, VMEM], [((feats, tokens), BF)], base, terms, chosen
    )
    return weight_in_grad[None], weight_out_grad[None], act_grad.T, gate_grad


def solution(mesh):
    return jax.shard_map(
        per_device,
        mesh=mesh,
        in_specs=(
            P("expert", "dp"),
            P("expert", "dp"),
            P("expert", None, "dp"),
            P("expert", "dp", None),
            P(),
            P("expert", None),
        ),
        out_specs=(
            P("expert", None, "dp"),
            P("expert", "dp", None),
            P("expert", "dp"),
            P("expert", None),
        ),
        check_vma=False,
    )
```

```python
import jax
import jax.numpy as jnp
from jax import lax
from jax.experimental import pallas as pl
from jax.experimental.pallas import tpu as pltpu
from jax.sharding import PartitionSpec as P

GELU_SCALE = 0.7978845608
CUBIC_COEF = 0.044715

NY, NZ = 8, 4
MIB = 1024 * 1024
BF, F32 = jnp.bfloat16, jnp.float32


def dp_index(y, z, core):
    return (y * NZ + z) * 2 + core


INNER = [[dp_index(y, z, 0) for y in range(NY)] for z in range(NZ)] + [
    [dp_index(2 * q + p, z, 1) for p in range(2) for z in range(NZ)] for q in range(4)
]
OUTER = [[dp_index(y, z, 0) for z in range(NZ)] for y in range(NY)] + [
    [dp_index(2 * q + p, z, 1) for q in range(4)] for p in range(2) for z in range(NZ)
]
EVERY_OTHER_Y = [
    [[dp_index(2 * q + p, z, c) for q in range(4)] for p in range(2) for z in range(NZ)]
    for c in range(2)
]
ALL_Z = [[[dp_index(y, z, c) for z in range(NZ)] for y in range(NY)] for c in range(2)]
FIRST = EVERY_OTHER_Y[0] + ALL_Z[1]
SECOND = ALL_Z[0] + EVERY_OTHER_Y[1]
NEIGHBOUR = [
    (dp_index(y, z, c), dp_index((y + (1 if y % 2 == c else NY - 1)) % NY, z, c))
    for y in range(NY)
    for z in range(NZ)
    for c in range(2)
]
SWAP = [(d, d ^ 1) for d in range(NY * NZ * 2)]


def gelu_parts(preact):
    inner = GELU_SCALE * (preact + CUBIC_COEF * preact * preact * preact)
    tanh_part = jnp.tanh(inner)
    gelu_val = 0.5 * preact * (1.0 + tanh_part)
    gelu_slope = 0.5 * (1.0 + tanh_part) + 0.5 * preact * (
        1.0 - tanh_part * tanh_part
    ) * GELU_SCALE * (1.0 + 3.0 * CUBIC_COEF * preact * preact)
    return gelu_val, gelu_slope


def contract(left, right, left_axis, right_axis):
    return lax.dot_general(
        left, right, (((left_axis,), (right_axis,)), ((), ())), preferred_element_type=F32
    )


def onehot(base, chosen_row, tokens):
    rows = chosen_row.shape[1]
    ids = base + lax.broadcasted_iota(jnp.int32, (tokens, rows), 0)
    return jnp.where(ids == chosen_row, 1.0, 0.0).astype(BF)


def hi_lo(value):
    high = value.astype(BF)
    low = (value - high.astype(F32)).astype(BF)
    return high, low


def pick_kernel(
    base_ref, act_hbm, grad_hbm, chosen_hbm, out_ref, both_ref, chosen_ref, sems
):
    feats = act_hbm.shape[0]
    copies = [
        pltpu.make_async_copy(act_hbm, both_ref.at[pl.ds(0, feats)], sems.at[0]),
        pltpu.make_async_copy(grad_hbm, both_ref.at[pl.ds(feats, feats)], sems.at[1]),
        pltpu.make_async_copy(chosen_hbm, chosen_ref, sems.at[2]),
    ]
    for copy in copies:
        copy.start()
    for copy in copies:
        copy.wait()
    both = both_ref[...]
    for e in range(out_ref.shape[0]):
        sel = onehot(base_ref[0], chosen_ref[e : e + 1, :], both.shape[1])
        out_ref[e] = contract(both, sel, 1, 0).astype(BF)


def merge_kernel(parts_ref, out_ref):
    total = parts_ref[0].astype(F32)
    for k in range(1, parts_ref.shape[0]):
        total = total + parts_ref[k].astype(F32)
    total = total.astype(BF)
    for k in range(out_ref.shape[0]):
        out_ref[k] = total


def gate_tile(pairs):
    rows = [half.astype(F32) for pair in pairs for half in pair]
    rows.append(jnp.zeros((16 - len(rows), rows[0].shape[1]), F32))
    return jnp.concatenate(rows, axis=0).astype(BF)


def block_rows(slots_ref, slot, feats):
    return pl.ds(pl.multiple_of(slots_ref[slot] * feats, feats), feats)


def load_blocks(slots_ref, first, blocks_ref, x_ref, u_ref, x_sem, u_sem):
    outer, inner, both = blocks_ref.shape[:3]
    feats = both // 2
    for o in range(outer):
        for i in range(inner):
            at = block_rows(slots_ref, first + o * inner + i, feats)
            act, grad = (blocks_ref.at[o, i, pl.ds(h * feats, feats)] for h in range(2))
            pltpu.make_async_copy(act, x_ref.at[at], x_sem).start()
            pltpu.make_async_copy(grad, u_ref.at[at], u_sem).start()
    half = pl.ds(0, outer * inner * feats)
    return (
        pltpu.make_async_copy(x_ref.at[half], x_ref.at[half], x_sem),
        pltpu.make_async_copy(u_ref.at[half], u_ref.at[half], u_sem),
    )


def ready_kernel(slots_ref, own_ref, w_in_ref, x_ref, u_ref, turned_ref, x_sem, u_sem):
    arrived = load_blocks(slots_ref, 0, own_ref, x_ref, u_ref, x_sem, u_sem)
    turned_ref[...] = w_in_ref[...].T
    for copy in arrived:
        copy.wait()


def more_kernel(slots_ref, oth_ref, pair_ref, x_in, u_in, x_ref, u_ref, x_sem, u_sem):
    count = pair_ref.shape[0] * pair_ref.shape[1]
    copies = []
    for k, ref in enumerate((oth_ref, pair_ref)):
        copies += load_blocks(slots_ref, (k + 1) * count, ref, x_ref, u_ref, x_sem.at[k], u_sem.at[k])
    for copy in copies:
        copy.wait()


def main_kernel(
    slots_ref, oth_ref, x_in, u_in, turned_ref, w_in_ref, w_out_ref, score_ref,
    x_ref, u_ref, back_ref, scaled_ref, gate_ref, send_ref, held_ref, x_sem, u_sem, w_sem,
):
    weights = pltpu.make_async_copy(w_out_ref, held_ref, w_sem)
    weights.start()
    count = oth_ref.shape[0] * oth_ref.shape[1]
    feats = oth_ref.shape[2] // 2
    x_done, u_done = load_blocks(slots_ref, 3 * count, oth_ref, x_ref, u_ref, x_sem, u_sem)
    x_done.wait()
    preact = contract(turned_ref[...], x_ref[...], 1, 0)
    u_done.wait()
    weights.wait()
    raw = contract(held_ref[...], u_ref[...], 1, 0)
    val, slope = gelu_parts(preact)
    hidden = val.astype(BF).astype(F32)
    score = score_ref[...]
    gate = jnp.sum(hidden * raw, axis=0, keepdims=True)
    back = (score * raw * slope).astype(BF)
    back_ref[...] = back
    scaled_ref[...] = (score * hidden).astype(BF)
    gate_ref[...] = gate
    slots = 2 * count
    for s in range(slots):
        at = block_rows(slots_ref, 3 * slots + s, feats)
        send_ref[pl.ds(s * feats, feats), :] = contract(w_in_ref[at, :], back, 1, 0).astype(BF)
    send_ref[pl.ds(slots * feats, 16), :] = gate_tile([hi_lo(gate)])


def weight_kernel(x_ref, u_ref, back_ref, scaled_ref, gin_ref, gout_ref):
    gin_ref[...] = contract(x_ref[...], back_ref[...], 1, 1).astype(BF)
    gout_ref[...] = contract(scaled_ref[...], u_ref[...], 1, 1).astype(BF)


def pair_kernel(slots_ref, w_in_ref, back_ref, gate_ref, got_ref, out_ref):
    parts, rows = out_ref.shape[0], out_ref.shape[1] - 16
    feats = rows // 8
    back = back_ref[...]
    tile = got_ref[pl.ds(parts * rows, 16), :].astype(F32)
    high, low = hi_lo(gate_ref[...])
    gate = (high.astype(F32) + low.astype(F32)) + (tile[0:1] + tile[1:2])
    packed = gate_tile([hi_lo(gate)])
    for k in range(parts):
        for i in range(8):
            s = k * 8 + i
            mine = contract(w_in_ref[block_rows(slots_ref, 2 * 8 * parts + s, feats), :], back, 1, 0)
            other = got_ref[pl.ds(s * feats, feats), :].astype(F32)
            out_ref[k, pl.ds(i * feats, feats), :] = (mine + other).astype(BF)
        out_ref[k, rows:, :] = packed


def outer_kernel(got_ref, out_ref):
    count, rows = out_ref.shape[0], out_ref.shape[1] - 16
    base = count * rows
    tiles = [got_ref[o, pl.ds(base, 16), :].astype(F32) for o in range(4)]
    packed = gate_tile([(t[0:1], t[1:2]) for t in tiles])
    for i in range(count):
        at = pl.ds(i * rows, rows)
        total = got_ref[0, at, :].astype(F32)
        for o in range(1, 4):
            total = total + got_ref[o, at, :].astype(F32)
        out_ref[i, :rows, :] = total.astype(BF)
        out_ref[i, rows:, :] = packed


def inner_kernel(core_ref, got_ref, out_ref, gate_ref):
    rows = out_ref.shape[1]
    sources = got_ref.shape[0]
    total = got_ref[0, :rows, :].astype(F32)
    for i in range(1, sources):
        total = total + got_ref[i, :rows, :].astype(F32)
    total = total.astype(BF)
    for k in range(out_ref.shape[0]):
        out_ref[k] = total
    tiles = [got_ref[i, rows:, :].astype(F32) for i in range(sources)]
    gates = [[t[2 * o : 2 * o + 1] + t[2 * o + 1 : 2 * o + 2] for o in range(4)] for t in tiles]
    first = core_ref[0] == 0
    gate = jnp.zeros((1, got_ref.shape[2]), F32)
    for y in range(NY):
        for z in range(NZ):
            gate = gate + jnp.where(first, gates[y][z], gates[(y % 2) * NZ + z][y // 2])
    gate_ref[...] = gate


def scatter_kernel(base_ref, terms_ref, chosen_ref, out_ref):
    tokens = out_ref.shape[1]
    total = jnp.zeros(out_ref.shape, F32)
    for e in range(terms_ref.shape[0]):
        sel = onehot(base_ref[0], chosen_ref[e : e + 1, :], tokens)
        total = total + contract(terms_ref[e], sel, 1, 1)
    out_ref[...] = total.astype(BF)


SMEM = pl.BlockSpec(memory_space=pltpu.SMEM)
VMEM = pl.BlockSpec(memory_space=pltpu.VMEM)
HBM = pl.BlockSpec(memory_space=pltpu.HBM)
ANY = pl.BlockSpec(memory_space=pl.ANY)


def call(kernel, specs, outs, *args, scratch=(), alias=None, mib=16, flops=0, moved=0):
    shapes = [jax.ShapeDtypeStruct(s, t) for s, t in outs]
    single = len(shapes) == 1
    return pl.pallas_call(
        kernel,
        out_shape=shapes[0] if single else shapes,
        in_specs=specs,
        out_specs=VMEM if single else [VMEM] * len(shapes),
        scratch_shapes=scratch,
        input_output_aliases=alias or {},
        cost_estimate=pl.CostEstimate(flops=flops, bytes_accessed=moved, transcendentals=0),
        compiler_params=pltpu.CompilerParams(vmem_limit_bytes=mib * MIB),
    )(*args)


def in_hbm(value):
    return pltpu.with_memory_space_constraint(value, pltpu.HBM)


def exchange(parts, axis, groups=None):
    return lax.all_to_all(parts, axis, 0, 0, axis_index_groups=groups)


def block_table(core):
    o = jnp.arange(4, dtype=jnp.int32)[:, None]
    i = jnp.arange(8, dtype=jnp.int32)[None, :]
    zero = dp_index(i, o, 0)
    one = dp_index(2 * o + i // NZ, i % NZ, 1)
    return jnp.where(core == 0, zero, one).reshape(-1)


def half_table(core, parity):
    o = jnp.arange(4, dtype=jnp.int32)[:, None]
    i = jnp.arange(4, dtype=jnp.int32)[None, :]
    zero = dp_index(2 * i + parity, o, 0)
    one = dp_index(2 * o + parity, i, 1)
    return jnp.where(core == 0, zero, one).reshape(-1)


def per_device(activations, out_grad, w_in, w_out, chosen, gate_scores):
    tokens, feats = activations.shape
    experts, rows = chosen.shape
    depth, units = w_in.shape[1], w_in.shape[2]
    base = (lax.axis_index("expert") * tokens).astype(jnp.int32).reshape(1)
    index = lax.axis_index("dp").astype(jnp.int32)
    core, parity = index & 1, (index >> 3) & 1
    slots = jnp.concatenate(
        [
            half_table(core, parity),
            half_table(1 - core, parity),
            half_table(core, 1 - parity),
            half_table(1 - core, 1 - parity),
            block_table(core),
            block_table(1 - core),
        ]
    )
    count = slots.shape[0] // 4

    picked = call(
        pick_kernel,
        [SMEM, HBM, HBM, HBM],
        [((experts, 2 * feats, rows), BF)],
        base, in_hbm(activations.T), in_hbm(out_grad.T), in_hbm(chosen),
        scratch=[
            pltpu.VMEM((2 * feats, tokens), BF),
            pltpu.VMEM((experts, rows), jnp.int32),
            pltpu.SemaphoreType.DMA((3,)),
        ],
    )
    picked = exchange(picked, "expert")
    mine = call(merge_kernel, [VMEM], [((4, 2 * feats, rows), BF)], picked)
    first = exchange(mine, "dp", FIRST)
    own = exchange(jnp.broadcast_to(first[None], (4,) + first.shape), "dp", SECOND)
    pair = lax.ppermute(own, "dp", NEIGHBOUR)
    near = lax.ppermute(own, "dp", SWAP)
    sems = [pltpu.SemaphoreType.DMA] * 2
    held = [((depth, rows), BF), ((depth, rows), BF)]
    x, u, turned = call(
        ready_kernel, [SMEM, ANY, VMEM], held + [((units, depth), BF)], slots, own, w_in[0],
        scratch=sems, flops=2 * MIB, moved=6 * MIB,
    )
    near, pair, x, u, turned = lax.optimization_barrier((near, pair, x, u, turned))
    other = lax.ppermute(pair, "dp", SWAP)
    x, u = call(
        more_kernel, [SMEM, ANY, ANY, VMEM, VMEM], held, slots, near, pair, x, u,
        scratch=[pltpu.SemaphoreType.DMA((2,))] * 2, alias={3: 0, 4: 1},
        flops=2 * MIB, moved=3 * MIB,
    )
    x, u, back, scaled, gate, send = call(
        main_kernel,
        [SMEM, ANY] + [VMEM] * 4 + [HBM, VMEM],
        held
        + [
            ((units, rows), BF),
            ((units, rows), BF),
            ((1, rows), F32),
            ((count * feats + 16, rows), BF),
        ],
        slots, other, x, u, turned, w_in[0], in_hbm(w_out[0]), gate_scores,
        scratch=[pltpu.VMEM((units, depth), BF)] + [pltpu.SemaphoreType.DMA] * 3, alias={2: 0, 3: 1},
    )
    got = lax.ppermute(send, "dp", SWAP)
    weight_grads = call(
        weight_kernel,
        [VMEM] * 4,
        [((depth, units), BF), ((units, depth), BF)],
        x, u, back, scaled, flops=4 * depth * units * rows, moved=6 * depth * rows,
    )
    got, weight_in_grad, weight_out_grad = lax.optimization_barrier((got, *weight_grads))
    part = call(
        pair_kernel,
        [SMEM] + [VMEM] * 4,
        [((4, 8 * feats + 16, rows), BF)],
        slots, w_in[0], back, gate, got,
    )
    part = exchange(part, "dp", OUTER)
    part = call(outer_kernel, [VMEM], [((8, feats + 16, rows), BF)], part)
    part = exchange(part, "dp", INNER)
    term, gate_grad = call(
        inner_kernel, [SMEM, VMEM], [((experts, feats, rows), BF), ((1, rows), F32)],
        core.reshape(1), part,
    )
    terms = exchange(term, "expert")
    act_grad = call(
        scatter_kernel, [SMEM, VMEM, VMEM], [((feats, tokens), BF)], base, terms, chosen
    )
    return weight_in_grad[None], weight_out_grad[None], act_grad.T, gate_grad


def solution(mesh):
    return jax.shard_map(
        per_device,
        mesh=mesh,
        in_specs=(
            P("expert", "dp"),
            P("expert", "dp"),
            P("expert", None, "dp"),
            P("expert", "dp", None),
            P(),
            P("expert", None),
        ),
        out_specs=(
            P("expert", None, "dp"),
            P("expert", "dp", None),
            P("expert", "dp"),
            P("expert", None),
        ),
        check_vma=False,
    )
```

```python
import jax
import jax.numpy as jnp
from jax import lax
from jax.experimental import pallas as pl
from jax.experimental.pallas import tpu as pltpu
from jax.sharding import PartitionSpec as P

GELU_SCALE = 0.7978845608
CUBIC_COEF = 0.044715

NY, NZ = 8, 4
MIB = 1024 * 1024
BF, F32 = jnp.bfloat16, jnp.float32


def dp_index(y, z, core):
    return (y * NZ + z) * 2 + core


EVERY_OTHER_Y = [
    [[dp_index(2 * q + p, z, c) for q in range(4)] for p in range(2) for z in range(NZ)]
    for c in range(2)
]
ALL_Z = [[[dp_index(y, z, c) for z in range(NZ)] for y in range(NY)] for c in range(2)]
FIRST = EVERY_OTHER_Y[0] + ALL_Z[1]
SECOND = ALL_Z[0] + EVERY_OTHER_Y[1]
NEIGHBOUR = [
    (dp_index(y, z, c), dp_index((y + (1 if y % 2 == c else NY - 1)) % NY, z, c))
    for y in range(NY)
    for z in range(NZ)
    for c in range(2)
]
SWAP = [(d, d ^ 1) for d in range(NY * NZ * 2)]


def gelu_parts(preact):
    inner = GELU_SCALE * (preact + CUBIC_COEF * preact * preact * preact)
    tanh_part = jnp.tanh(inner)
    gelu_val = 0.5 * preact * (1.0 + tanh_part)
    gelu_slope = 0.5 * (1.0 + tanh_part) + 0.5 * preact * (
        1.0 - tanh_part * tanh_part
    ) * GELU_SCALE * (1.0 + 3.0 * CUBIC_COEF * preact * preact)
    return gelu_val, gelu_slope


def contract(left, right, left_axis, right_axis):
    return lax.dot_general(
        left, right, (((left_axis,), (right_axis,)), ((), ())), preferred_element_type=F32
    )


def onehot(base, chosen_row, tokens):
    rows = chosen_row.shape[1]
    ids = base + lax.broadcasted_iota(jnp.int32, (tokens, rows), 0)
    return jnp.where(ids == chosen_row, 1.0, 0.0).astype(BF)


def hi_lo(value):
    high = value.astype(BF)
    low = (value - high.astype(F32)).astype(BF)
    return high, low


def pick_kernel(
    base_ref, act_hbm, grad_hbm, chosen_hbm, out_ref, both_ref, chosen_ref, sems
):
    feats = act_hbm.shape[0]
    copies = [
        pltpu.make_async_copy(act_hbm, both_ref.at[pl.ds(0, feats)], sems.at[0]),
        pltpu.make_async_copy(grad_hbm, both_ref.at[pl.ds(feats, feats)], sems.at[1]),
        pltpu.make_async_copy(chosen_hbm, chosen_ref, sems.at[2]),
    ]
    for copy in copies:
        copy.start()
    for copy in copies:
        copy.wait()
    both = both_ref[...]
    for e in range(out_ref.shape[0]):
        sel = onehot(base_ref[0], chosen_ref[e : e + 1, :], both.shape[1])
        out_ref[e] = contract(both, sel, 1, 0).astype(BF)


def merge_kernel(parts_ref, out_ref):
    total = parts_ref[0].astype(F32)
    for k in range(1, parts_ref.shape[0]):
        total = total + parts_ref[k].astype(F32)
    total = total.astype(BF)
    for k in range(out_ref.shape[0]):
        out_ref[k] = total


def gate_tile(pairs):
    rows = [half.astype(F32) for pair in pairs for half in pair]
    rows.append(jnp.zeros((16 - len(rows), rows[0].shape[1]), F32))
    return jnp.concatenate(rows, axis=0).astype(BF)


def block_rows(slots_ref, slot, feats):
    return pl.ds(pl.multiple_of(slots_ref[slot] * feats, feats), feats)


def load_blocks(slots_ref, first, blocks_ref, x_ref, u_ref, x_sem, u_sem):
    outer, inner, both = blocks_ref.shape[:3]
    feats = both // 2
    for o in range(outer):
        for i in range(inner):
            at = block_rows(slots_ref, first + o * inner + i, feats)
            act, grad = (blocks_ref.at[o, i, pl.ds(h * feats, feats)] for h in range(2))
            pltpu.make_async_copy(act, x_ref.at[at], x_sem).start()
            pltpu.make_async_copy(grad, u_ref.at[at], u_sem).start()
    half = pl.ds(0, outer * inner * feats)
    return (
        pltpu.make_async_copy(x_ref.at[half], x_ref.at[half], x_sem),
        pltpu.make_async_copy(u_ref.at[half], u_ref.at[half], u_sem),
    )


def ready_kernel(slots_ref, own_ref, w_in_ref, x_ref, u_ref, turned_ref, x_sem, u_sem):
    arrived = load_blocks(slots_ref, 0, own_ref, x_ref, u_ref, x_sem, u_sem)
    turned_ref[...] = w_in_ref[...].T
    for copy in arrived:
        copy.wait()


def more_kernel(slots_ref, oth_ref, pair_ref, x_in, u_in, x_ref, u_ref, x_sem, u_sem):
    count = pair_ref.shape[0] * pair_ref.shape[1]
    copies = []
    for k, ref in enumerate((oth_ref, pair_ref)):
        copies += load_blocks(slots_ref, (k + 1) * count, ref, x_ref, u_ref, x_sem.at[k], u_sem.at[k])
    for copy in copies:
        copy.wait()


def main_kernel(
    slots_ref, oth_ref, x_in, u_in, turned_ref, w_in_ref, w_out_ref, score_ref,
    x_ref, u_ref, back_ref, scaled_ref, gate_ref, send_ref, held_ref, x_sem, u_sem, w_sem,
):
    weights = pltpu.make_async_copy(w_out_ref, held_ref, w_sem)
    weights.start()
    count = oth_ref.shape[0] * oth_ref.shape[1]
    feats = oth_ref.shape[2] // 2
    x_done, u_done = load_blocks(slots_ref, 3 * count, oth_ref, x_ref, u_ref, x_sem, u_sem)
    x_done.wait()
    preact = contract(turned_ref[...], x_ref[...], 1, 0)
    u_done.wait()
    weights.wait()
    raw = contract(held_ref[...], u_ref[...], 1, 0)
    val, slope = gelu_parts(preact)
    hidden = val.astype(BF).astype(F32)
    score = score_ref[...]
    gate = jnp.sum(hidden * raw, axis=0, keepdims=True)
    back = (score * raw * slope).astype(BF)
    back_ref[...] = back
    scaled_ref[...] = (score * hidden).astype(BF)
    gate_ref[...] = gate
    slots = 2 * count
    for s in range(slots):
        at = block_rows(slots_ref, s + count * (1 + s // count), feats)
        send_ref[pl.ds(s * feats, feats), :] = contract(w_in_ref[at, :], back, 1, 0).astype(BF)
    send_ref[pl.ds(slots * feats, 16), :] = gate_tile([hi_lo(gate)])


def weight_kernel(x_ref, u_ref, back_ref, scaled_ref, gin_ref, gout_ref):
    gin_ref[...] = contract(x_ref[...], back_ref[...], 1, 1).astype(BF)
    gout_ref[...] = contract(scaled_ref[...], u_ref[...], 1, 1).astype(BF)


def add_blocks(slots_ref, first, w_in_ref, back, got_ref, base, out_ref):
    feats = 64
    for s in range(16):
        mine = contract(w_in_ref[block_rows(slots_ref, first + s, feats), :], back, 1, 0)
        other = got_ref[pl.ds(base + s * feats, feats), :].astype(F32)
        out_ref[pl.ds(s * feats, feats), :] = (mine + other).astype(out_ref.dtype)


def far_kernel(slots_ref, w_in_ref, back_ref, gate_ref, got_ref, far_ref):
    rows = far_ref.shape[0] - 16
    add_blocks(slots_ref, 32, w_in_ref, back_ref[...], got_ref, rows, far_ref)
    tile = got_ref[pl.ds(2 * rows, 16), :].astype(F32)
    high, low = hi_lo(gate_ref[...])
    gate = (high.astype(F32) + low.astype(F32)) + (tile[0:1] + tile[1:2])
    far_ref[pl.ds(rows, 16), :] = gate_tile([hi_lo(gate)])


def near_kernel(slots_ref, w_in_ref, back_ref, got_ref, near_ref):
    add_blocks(slots_ref, 0, w_in_ref, back_ref[...], got_ref, 0, near_ref)


def join_kernel(near_ref, far_ref, got_ref, out_ref):
    parts, rows = out_ref.shape[0], out_ref.shape[1] - 16
    tiles = [ref[pl.ds(parts * rows, 16), :].astype(F32) for ref in (far_ref, got_ref)]
    packed = gate_tile([(t[0:1], t[1:2]) for t in tiles])
    for k in range(parts):
        at = pl.ds(k * rows, rows)
        out_ref[k, :rows, :] = (near_ref[at, :] + got_ref[at, :].astype(F32)).astype(BF)
        out_ref[k, rows:, :] = packed


def outer_kernel(got_ref, out_ref):
    count, rows = out_ref.shape[0], out_ref.shape[1] - 16
    base = count * rows
    tiles = [got_ref[o, pl.ds(base, 16), :].astype(F32) for o in range(4)]
    packed = jnp.concatenate([t[0:4] for t in tiles], axis=0).astype(BF)
    for i in range(count):
        at = pl.ds(i * rows, rows)
        total = got_ref[0, at, :].astype(F32)
        for o in range(1, 4):
            total = total + got_ref[o, at, :].astype(F32)
        out_ref[i, :rows, :] = total.astype(BF)
        out_ref[i, rows:, :] = packed


def gate_source(core, parity, y, z):
    odd = y % 2
    if core == 0:
        return y // 2, z, odd ^ parity
    if odd == parity:
        return z, y // 2, 0
    return z, ((y + 1) // 2 if parity == 0 else (y + 6) // 2) % 4, 1


def inner_kernel(place_ref, got_ref, out_ref, gate_ref):
    rows = out_ref.shape[1]
    sources = got_ref.shape[0]
    total = got_ref[0, :rows, :].astype(F32)
    for i in range(1, sources):
        total = total + got_ref[i, :rows, :].astype(F32)
    total = total.astype(BF)
    for k in range(out_ref.shape[0]):
        out_ref[k] = total
    tiles = [got_ref[i, rows:, :].astype(F32) for i in range(sources)]
    gates = [[t[2 * j : 2 * j + 1] + t[2 * j + 1 : 2 * j + 2] for j in range(8)] for t in tiles]
    place = place_ref[0]
    gate = jnp.zeros((1, got_ref.shape[2]), F32)
    for y in range(NY):
        for z in range(NZ):
            term = None
            for core in range(2):
                for parity in range(2):
                    i, o, n = gate_source(core, parity, y, z)
                    value = gates[i][2 * o + n]
                    here = place == 2 * core + parity
                    term = value if term is None else jnp.where(here, value, term)
            gate = gate + term
    gate_ref[...] = gate


def scatter_kernel(base_ref, terms_ref, chosen_ref, out_ref):
    tokens = out_ref.shape[1]
    total = jnp.zeros(out_ref.shape, F32)
    for e in range(terms_ref.shape[0]):
        sel = onehot(base_ref[0], chosen_ref[e : e + 1, :], tokens)
        total = total + contract(terms_ref[e], sel, 1, 1)
    out_ref[...] = total.astype(BF)


SMEM = pl.BlockSpec(memory_space=pltpu.SMEM)
VMEM = pl.BlockSpec(memory_space=pltpu.VMEM)
HBM = pl.BlockSpec(memory_space=pltpu.HBM)
ANY = pl.BlockSpec(memory_space=pl.ANY)


def call(kernel, specs, outs, *args, scratch=(), alias=None, mib=16, flops=0, moved=0):
    shapes = [jax.ShapeDtypeStruct(s, t) for s, t in outs]
    single = len(shapes) == 1
    return pl.pallas_call(
        kernel,
        out_shape=shapes[0] if single else shapes,
        in_specs=specs,
        out_specs=VMEM if single else [VMEM] * len(shapes),
        scratch_shapes=scratch,
        input_output_aliases=alias or {},
        cost_estimate=pl.CostEstimate(flops=flops, bytes_accessed=moved, transcendentals=0),
        compiler_params=pltpu.CompilerParams(vmem_limit_bytes=mib * MIB),
    )(*args)


def in_hbm(value):
    return pltpu.with_memory_space_constraint(value, pltpu.HBM)


def exchange(parts, axis, groups=None):
    return lax.all_to_all(parts, axis, 0, 0, axis_index_groups=groups)


def half_table(core, parity):
    o = jnp.arange(4, dtype=jnp.int32)[:, None]
    i = jnp.arange(4, dtype=jnp.int32)[None, :]
    zero = dp_index(2 * i + parity, o, 0)
    one = dp_index(2 * o + parity, i, 1)
    return jnp.where(core == 0, zero, one).reshape(-1)


def per_device(activations, out_grad, w_in, w_out, chosen, gate_scores):
    tokens, feats = activations.shape
    experts, rows = chosen.shape
    depth, units = w_in.shape[1], w_in.shape[2]
    base = (lax.axis_index("expert") * tokens).astype(jnp.int32).reshape(1)
    index = lax.axis_index("dp").astype(jnp.int32)
    core, parity = index & 1, (index >> 3) & 1
    slots = jnp.concatenate(
        [
            half_table(core, parity),
            half_table(1 - core, parity),
            half_table(core, 1 - parity),
            half_table(1 - core, 1 - parity),
        ]
    )
    count = slots.shape[0] // 2

    picked = call(
        pick_kernel,
        [SMEM, HBM, HBM, HBM],
        [((experts, 2 * feats, rows), BF)],
        base, in_hbm(activations.T), in_hbm(out_grad.T), in_hbm(chosen),
        scratch=[
            pltpu.VMEM((2 * feats, tokens), BF),
            pltpu.VMEM((experts, rows), jnp.int32),
            pltpu.SemaphoreType.DMA((3,)),
        ],
    )
    picked = exchange(picked, "expert")
    mine = call(merge_kernel, [VMEM], [((4, 2 * feats, rows), BF)], picked)
    first = exchange(mine, "dp", FIRST)
    own = exchange(jnp.broadcast_to(first[None], (4,) + first.shape), "dp", SECOND)
    pair = lax.ppermute(own, "dp", NEIGHBOUR)
    near = lax.ppermute(own, "dp", SWAP)
    sems = [pltpu.SemaphoreType.DMA] * 2
    held = [((depth, rows), BF), ((depth, rows), BF)]
    x, u, turned = call(
        ready_kernel, [SMEM, ANY, VMEM], held + [((units, depth), BF)], slots, own, w_in[0],
        scratch=sems, flops=2 * MIB, moved=6 * MIB,
    )
    near, pair, x, u, turned = lax.optimization_barrier((near, pair, x, u, turned))
    other = lax.ppermute(pair, "dp", SWAP)
    x, u = call(
        more_kernel, [SMEM, ANY, ANY, VMEM, VMEM], held, slots, near, pair, x, u,
        scratch=[pltpu.SemaphoreType.DMA((2,))] * 2, alias={3: 0, 4: 1},
        flops=2 * MIB, moved=3 * MIB,
    )
    x, u, back, scaled, gate, send = call(
        main_kernel,
        [SMEM, ANY] + [VMEM] * 4 + [HBM, VMEM],
        held
        + [
            ((units, rows), BF),
            ((units, rows), BF),
            ((1, rows), F32),
            ((count * feats + 16, rows), BF),
        ],
        slots, other, x, u, turned, w_in[0], in_hbm(w_out[0]), gate_scores,
        scratch=[pltpu.VMEM((units, depth), BF)] + [pltpu.SemaphoreType.DMA] * 3, alias={2: 0, 3: 1},
    )
    got = lax.ppermute(send, "dp", SWAP)
    weight_grads = call(
        weight_kernel,
        [VMEM] * 4,
        [((depth, units), BF), ((units, depth), BF)],
        x, u, back, scaled, flops=4 * depth * units * rows, moved=6 * depth * rows,
    )
    got, weight_in_grad, weight_out_grad = lax.optimization_barrier((got, *weight_grads))
    half = count * feats // 2
    far = call(
        far_kernel, [SMEM] + [VMEM] * 4, [((half + 16, rows), BF)],
        slots, w_in[0], back, gate, got,
    )
    come = lax.ppermute(far, "dp", NEIGHBOUR)
    near = call(
        near_kernel, [SMEM] + [VMEM] * 3, [((half, rows), F32)], slots, w_in[0], back, got,
        flops=depth * units * rows // 2, moved=4 * MIB,
    )
    near, come = lax.optimization_barrier((near, come))
    part = call(join_kernel, [VMEM] * 3, [((4, 4 * feats + 16, rows), BF)], near, far, come)
    part = exchange(part, "dp", SECOND)
    part = call(outer_kernel, [VMEM], [((4, feats + 16, rows), BF)], part)
    part = exchange(part, "dp", FIRST)
    term, gate_grad = call(
        inner_kernel, [SMEM, VMEM], [((experts, feats, rows), BF), ((1, rows), F32)],
        (2 * core + parity).reshape(1), part,
    )
    terms = exchange(term, "expert")
    act_grad = call(
        scatter_kernel, [SMEM, VMEM, VMEM], [((feats, tokens), BF)], base, terms, chosen
    )
    return weight_in_grad[None], weight_out_grad[None], act_grad.T, gate_grad


def solution(mesh):
    return jax.shard_map(
        per_device,
        mesh=mesh,
        in_specs=(
            P("expert", "dp"),
            P("expert", "dp"),
            P("expert", None, "dp"),
            P("expert", "dp", None),
            P(),
            P("expert", None),
        ),
        out_specs=(
            P("expert", None, "dp"),
            P("expert", "dp", None),
            P("expert", "dp"),
            P("expert", None),
        ),
        check_vma=False,
    )
```

```python
import jax
import jax.numpy as jnp
from jax import lax
from jax.experimental import pallas as pl
from jax.experimental.pallas import tpu as pltpu
from jax.sharding import PartitionSpec as P

GELU_SCALE = 0.7978845608
CUBIC_COEF = 0.044715

NY, NZ = 8, 4
MIB = 1024 * 1024
BF, F32 = jnp.bfloat16, jnp.float32


def dp_index(y, z, core):
    return (y * NZ + z) * 2 + core


INNER = [[dp_index(y, z, 0) for y in range(NY)] for z in range(NZ)] + [
    [dp_index(2 * q + p, z, 1) for p in range(2) for z in range(NZ)] for q in range(4)
]
OUTER = [[dp_index(y, z, 0) for z in range(NZ)] for y in range(NY)] + [
    [dp_index(2 * q + p, z, 1) for q in range(4)] for p in range(2) for z in range(NZ)
]
EVERY_OTHER_Y = [
    [[dp_index(2 * q + p, z, c) for q in range(4)] for p in range(2) for z in range(NZ)]
    for c in range(2)
]
ALL_Z = [[[dp_index(y, z, c) for z in range(NZ)] for y in range(NY)] for c in range(2)]
FIRST = EVERY_OTHER_Y[0] + ALL_Z[1]
SECOND = ALL_Z[0] + EVERY_OTHER_Y[1]
NEIGHBOUR = [
    (dp_index(y, z, c), dp_index((y + (1 if y % 2 == c else NY - 1)) % NY, z, c))
    for y in range(NY)
    for z in range(NZ)
    for c in range(2)
]
SWAP = [(d, d ^ 1) for d in range(NY * NZ * 2)]


def gelu_parts(preact):
    inner = GELU_SCALE * (preact + CUBIC_COEF * preact * preact * preact)
    tanh_part = jnp.tanh(inner)
    gelu_val = 0.5 * preact * (1.0 + tanh_part)
    gelu_slope = 0.5 * (1.0 + tanh_part) + 0.5 * preact * (
        1.0 - tanh_part * tanh_part
    ) * GELU_SCALE * (1.0 + 3.0 * CUBIC_COEF * preact * preact)
    return gelu_val, gelu_slope


def contract(left, right, left_axis, right_axis):
    return lax.dot_general(
        left, right, (((left_axis,), (right_axis,)), ((), ())), preferred_element_type=F32
    )


def onehot(base, chosen_row, tokens):
    rows = chosen_row.shape[1]
    ids = base + lax.broadcasted_iota(jnp.int32, (tokens, rows), 0)
    return jnp.where(ids == chosen_row, 1.0, 0.0).astype(BF)


def hi_lo(value):
    high = value.astype(BF)
    low = (value - high.astype(F32)).astype(BF)
    return high, low


def pick_kernel(
    base_ref, act_hbm, grad_hbm, chosen_hbm, out_ref, both_ref, chosen_ref, sems
):
    feats = act_hbm.shape[0]
    copies = [
        pltpu.make_async_copy(act_hbm, both_ref.at[pl.ds(0, feats)], sems.at[0]),
        pltpu.make_async_copy(grad_hbm, both_ref.at[pl.ds(feats, feats)], sems.at[1]),
        pltpu.make_async_copy(chosen_hbm, chosen_ref, sems.at[2]),
    ]
    for copy in copies:
        copy.start()
    for copy in copies:
        copy.wait()
    both = both_ref[...]
    for e in range(out_ref.shape[0]):
        sel = onehot(base_ref[0], chosen_ref[e : e + 1, :], both.shape[1])
        out_ref[e] = contract(both, sel, 1, 0).astype(BF)


def merge_kernel(parts_ref, out_ref):
    total = parts_ref[0].astype(F32)
    for k in range(1, parts_ref.shape[0]):
        total = total + parts_ref[k].astype(F32)
    total = total.astype(BF)
    for k in range(out_ref.shape[0]):
        out_ref[k] = total


def gate_tile(pairs):
    rows = [half.astype(F32) for pair in pairs for half in pair]
    rows.append(jnp.zeros((16 - len(rows), rows[0].shape[1]), F32))
    return jnp.concatenate(rows, axis=0).astype(BF)


def block_rows(slots_ref, slot, feats):
    return pl.ds(pl.multiple_of(slots_ref[slot] * feats, feats), feats)


def load_blocks(slots_ref, first, blocks_ref, x_ref, u_ref, x_sem, u_sem):
    outer, inner, both = blocks_ref.shape[:3]
    feats = both // 2
    for o in range(outer):
        for i in range(inner):
            at = block_rows(slots_ref, first + o * inner + i, feats)
            act, grad = (blocks_ref.at[o, i, pl.ds(h * feats, feats)] for h in range(2))
            pltpu.make_async_copy(act, x_ref.at[at], x_sem).start()
            pltpu.make_async_copy(grad, u_ref.at[at], u_sem).start()
    half = pl.ds(0, outer * inner * feats)
    return (
        pltpu.make_async_copy(x_ref.at[half], x_ref.at[half], x_sem),
        pltpu.make_async_copy(u_ref.at[half], u_ref.at[half], u_sem),
    )


def ready_kernel(
    slots_ref, own_ref, w_in_ref, w_out_ref,
    x_ref, u_ref, turned_ref, order_ref, held_ref, x_sem, u_sem, w_sem,
):
    weights = pltpu.make_async_copy(w_out_ref, held_ref, w_sem)
    weights.start()
    arrived = load_blocks(slots_ref, 0, own_ref, x_ref, u_ref, x_sem, u_sem) + (weights,)
    turned_ref[...] = w_in_ref[...].T
    count, feats = slots_ref.shape[0] // 2, own_ref.shape[2] // 2
    for s in range(count):
        at = block_rows(slots_ref, count + s, feats)
        order_ref[pl.ds(s * feats, feats), :] = w_in_ref[at, :]
    for copy in arrived:
        copy.wait()


def more_kernel(slots_ref, oth_ref, pair_ref, x_in, u_in, x_ref, u_ref, x_sem, u_sem):
    count = pair_ref.shape[0] * pair_ref.shape[1]
    copies = []
    for k, ref in enumerate((oth_ref, pair_ref)):
        copies += load_blocks(slots_ref, (k + 1) * count, ref, x_ref, u_ref, x_sem.at[k], u_sem.at[k])
    for copy in copies:
        copy.wait()


def main_kernel(
    slots_ref, oth_ref, x_in, u_in, turned_ref, order_ref, w_out_ref, score_ref,
    x_ref, u_ref, back_ref, scaled_ref, gate_ref, send_ref, x_sem, u_sem,
):
    count = oth_ref.shape[0] * oth_ref.shape[1]
    x_done, u_done = load_blocks(slots_ref, 3 * count, oth_ref, x_ref, u_ref, x_sem, u_sem)
    x_done.wait()
    preact = contract(turned_ref[...], x_ref[...], 1, 0)
    u_done.wait()
    raw = contract(w_out_ref[...], u_ref[...], 1, 0)
    val, slope = gelu_parts(preact)
    hidden = val.astype(BF).astype(F32)
    score = score_ref[...]
    gate = jnp.sum(hidden * raw, axis=0, keepdims=True)
    back = (score * raw * slope).astype(BF)
    back_ref[...] = back
    scaled_ref[...] = (score * hidden).astype(BF)
    gate_ref[...] = gate
    half = order_ref.shape[0] // 2
    send = contract(order_ref[pl.ds(half, half), :], back, 1, 0)
    send_ref[pl.ds(0, half), :] = send.astype(BF)
    send_ref[pl.ds(half, 16), :] = gate_tile([hi_lo(gate)])


def weight_kernel(x_ref, u_ref, back_ref, scaled_ref, gin_ref, gout_ref):
    gin_ref[...] = contract(x_ref[...], back_ref[...], 1, 1).astype(BF)
    gout_ref[...] = contract(scaled_ref[...], u_ref[...], 1, 1).astype(BF)


def pair_kernel(order_ref, back_ref, gate_ref, got_ref, out_ref):
    parts, rows = out_ref.shape[0], out_ref.shape[1] - 16
    back = back_ref[...]
    tile = got_ref[pl.ds(parts * rows, 16), :].astype(F32)
    high, low = hi_lo(gate_ref[...])
    gate = (high.astype(F32) + low.astype(F32)) + (tile[0:1] + tile[1:2])
    packed = gate_tile([hi_lo(gate)])
    for k in range(parts):
        at = pl.ds(k * rows, rows)
        mine = contract(order_ref[at, :], back, 1, 0)
        out_ref[k, :rows, :] = (mine + got_ref[at, :].astype(F32)).astype(BF)
        out_ref[k, rows:, :] = packed


def outer_kernel(got_ref, out_ref):
    count, rows = out_ref.shape[0], out_ref.shape[1] - 16
    base = count * rows
    tiles = [got_ref[o, pl.ds(base, 16), :].astype(F32) for o in range(4)]
    packed = gate_tile([(t[0:1], t[1:2]) for t in tiles])
    for i in range(count):
        at = pl.ds(i * rows, rows)
        total = got_ref[0, at, :].astype(F32)
        for o in range(1, 4):
            total = total + got_ref[o, at, :].astype(F32)
        out_ref[i, :rows, :] = total.astype(BF)
        out_ref[i, rows:, :] = packed


def inner_kernel(core_ref, got_ref, out_ref, gate_ref):
    rows = out_ref.shape[1]
    sources = got_ref.shape[0]
    total = got_ref[0, :rows, :].astype(F32)
    for i in range(1, sources):
        total = total + got_ref[i, :rows, :].astype(F32)
    total = total.astype(BF)
    for k in range(out_ref.shape[0]):
        out_ref[k] = total
    tiles = [got_ref[i, rows:, :].astype(F32) for i in range(sources)]
    gates = [[t[2 * o : 2 * o + 1] + t[2 * o + 1 : 2 * o + 2] for o in range(4)] for t in tiles]
    first = core_ref[0] == 0
    gate = jnp.zeros((1, got_ref.shape[2]), F32)
    for y in range(NY):
        for z in range(NZ):
            gate = gate + jnp.where(first, gates[y][z], gates[(y % 2) * NZ + z][y // 2])
    gate_ref[...] = gate


def scatter_kernel(base_ref, terms_ref, chosen_ref, out_ref):
    tokens = out_ref.shape[1]
    total = jnp.zeros(out_ref.shape, F32)
    for e in range(terms_ref.shape[0]):
        sel = onehot(base_ref[0], chosen_ref[e : e + 1, :], tokens)
        total = total + contract(terms_ref[e], sel, 1, 1)
    out_ref[...] = total.astype(BF)


SMEM = pl.BlockSpec(memory_space=pltpu.SMEM)
VMEM = pl.BlockSpec(memory_space=pltpu.VMEM)
HBM = pl.BlockSpec(memory_space=pltpu.HBM)
ANY = pl.BlockSpec(memory_space=pl.ANY)


def call(kernel, specs, outs, *args, scratch=(), alias=None, mib=16, flops=0, moved=0):
    shapes = [jax.ShapeDtypeStruct(s, t) for s, t in outs]
    single = len(shapes) == 1
    return pl.pallas_call(
        kernel,
        out_shape=shapes[0] if single else shapes,
        in_specs=specs,
        out_specs=VMEM if single else [VMEM] * len(shapes),
        scratch_shapes=scratch,
        input_output_aliases=alias or {},
        cost_estimate=pl.CostEstimate(flops=flops, bytes_accessed=moved, transcendentals=0),
        compiler_params=pltpu.CompilerParams(vmem_limit_bytes=mib * MIB),
    )(*args)


def in_hbm(value):
    return pltpu.with_memory_space_constraint(value, pltpu.HBM)


def exchange(parts, axis, groups=None):
    return lax.all_to_all(parts, axis, 0, 0, axis_index_groups=groups)


def block_table(core):
    o = jnp.arange(4, dtype=jnp.int32)[:, None]
    i = jnp.arange(8, dtype=jnp.int32)[None, :]
    zero = dp_index(i, o, 0)
    one = dp_index(2 * o + i // NZ, i % NZ, 1)
    return jnp.where(core == 0, zero, one).reshape(-1)


def half_table(core, parity):
    o = jnp.arange(4, dtype=jnp.int32)[:, None]
    i = jnp.arange(4, dtype=jnp.int32)[None, :]
    zero = dp_index(2 * i + parity, o, 0)
    one = dp_index(2 * o + parity, i, 1)
    return jnp.where(core == 0, zero, one).reshape(-1)


def per_device(activations, out_grad, w_in, w_out, chosen, gate_scores):
    tokens, feats = activations.shape
    experts, rows = chosen.shape
    depth, units = w_in.shape[1], w_in.shape[2]
    base = (lax.axis_index("expert") * tokens).astype(jnp.int32).reshape(1)
    index = lax.axis_index("dp").astype(jnp.int32)
    core, parity = index & 1, (index >> 3) & 1
    slots = jnp.concatenate(
        [
            half_table(core, parity),
            half_table(1 - core, parity),
            half_table(core, 1 - parity),
            half_table(1 - core, 1 - parity),
            block_table(core),
            block_table(1 - core),
        ]
    )
    count = slots.shape[0] // 4

    picked = call(
        pick_kernel,
        [SMEM, HBM, HBM, HBM],
        [((experts, 2 * feats, rows), BF)],
        base, in_hbm(activations.T), in_hbm(out_grad.T), in_hbm(chosen),
        scratch=[
            pltpu.VMEM((2 * feats, tokens), BF),
            pltpu.VMEM((experts, rows), jnp.int32),
            pltpu.SemaphoreType.DMA((3,)),
        ],
    )
    picked = exchange(picked, "expert")
    mine = call(merge_kernel, [VMEM], [((4, 2 * feats, rows), BF)], picked)
    first = exchange(mine, "dp", FIRST)
    own = exchange(jnp.broadcast_to(first[None], (4,) + first.shape), "dp", SECOND)
    pair = lax.ppermute(own, "dp", NEIGHBOUR)
    near = lax.ppermute(own, "dp", SWAP)
    sems = [pltpu.SemaphoreType.DMA] * 2
    held = [((depth, rows), BF), ((depth, rows), BF)]
    weight = ((depth, units), BF)
    x, u, turned, order, held_out = call(
        ready_kernel, [SMEM, ANY, VMEM, HBM], held + [((units, depth), BF), weight, ((units, depth), BF)],
        slots, own, w_in[0], in_hbm(w_out[0]),
        scratch=sems + sems[:1], flops=2 * MIB, moved=6 * MIB,
    )
    near, pair, x, u, turned = lax.optimization_barrier((near, pair, x, u, turned))
    other = lax.ppermute(pair, "dp", SWAP)
    x, u = call(
        more_kernel, [SMEM, ANY, ANY, VMEM, VMEM], held, slots, near, pair, x, u,
        scratch=[pltpu.SemaphoreType.DMA((2,))] * 2, alias={3: 0, 4: 1},
        flops=2 * MIB, moved=3 * MIB,
    )
    x, u, back, scaled, gate, send = call(
        main_kernel,
        [SMEM, ANY] + [VMEM] * 6,
        held
        + [
            ((units, rows), BF),
            ((units, rows), BF),
            ((1, rows), F32),
            ((count * feats + 16, rows), BF),
        ],
        slots, other, x, u, turned, order, held_out, gate_scores,
        scratch=sems, alias={2: 0, 3: 1},
    )
    got = lax.ppermute(send, "dp", SWAP)
    weight_grads = call(
        weight_kernel,
        [VMEM] * 4,
        [((depth, units), BF), ((units, depth), BF)],
        x, u, back, scaled, flops=4 * depth * units * rows, moved=6 * depth * rows,
    )
    got, weight_in_grad, weight_out_grad = lax.optimization_barrier((got, *weight_grads))
    part = call(
        pair_kernel,
        [VMEM] * 4,
        [((4, 8 * feats + 16, rows), BF)],
        order, back, gate, got,
    )
    part = exchange(part, "dp", OUTER)
    part = call(outer_kernel, [VMEM], [((8, feats + 16, rows), BF)], part)
    part = exchange(part, "dp", INNER)
    term, gate_grad = call(
        inner_kernel, [SMEM, VMEM], [((experts, feats, rows), BF), ((1, rows), F32)],
        core.reshape(1), part,
    )
    terms = exchange(term, "expert")
    act_grad = call(
        scatter_kernel, [SMEM, VMEM, VMEM], [((feats, tokens), BF)], base, terms, chosen
    )
    return weight_in_grad[None], weight_out_grad[None], act_grad.T, gate_grad


def solution(mesh):
    return jax.shard_map(
        per_device,
        mesh=mesh,
        in_specs=(
            P("expert", "dp"),
            P("expert", "dp"),
            P("expert", None, "dp"),
            P("expert", "dp", None),
            P(),
            P("expert", None),
        ),
        out_specs=(
            P("expert", None, "dp"),
            P("expert", "dp", None),
            P("expert", "dp"),
            P("expert", None),
        ),
        check_vma=False,
    )
```

```python
import jax
import jax.numpy as jnp
from jax import lax
from jax.experimental import pallas as pl
from jax.experimental.pallas import tpu as pltpu
from jax.sharding import PartitionSpec as P

GELU_SCALE = 0.7978845608
CUBIC_COEF = 0.044715

NY, NZ = 8, 4
MIB = 1024 * 1024
BF, F32 = jnp.bfloat16, jnp.float32


def dp_index(y, z, core):
    return (y * NZ + z) * 2 + core


INNER = [[dp_index(y, z, 0) for y in range(NY)] for z in range(NZ)] + [
    [dp_index(2 * q + p, z, 1) for p in range(2) for z in range(NZ)] for q in range(4)
]
OUTER = [[dp_index(y, z, 0) for z in range(NZ)] for y in range(NY)] + [
    [dp_index(2 * q + p, z, 1) for q in range(4)] for p in range(2) for z in range(NZ)
]
EVERY_OTHER_Y = [
    [[dp_index(2 * q + p, z, c) for q in range(4)] for p in range(2) for z in range(NZ)]
    for c in range(2)
]
ALL_Z = [[[dp_index(y, z, c) for z in range(NZ)] for y in range(NY)] for c in range(2)]
FIRST = EVERY_OTHER_Y[0] + ALL_Z[1]
SECOND = ALL_Z[0] + EVERY_OTHER_Y[1]
NEIGHBOUR = [
    (dp_index(y, z, c), dp_index((y + (1 if y % 2 == c else NY - 1)) % NY, z, c))
    for y in range(NY)
    for z in range(NZ)
    for c in range(2)
]
SWAP = [(d, d ^ 1) for d in range(NY * NZ * 2)]


def gelu_parts(preact):
    inner = GELU_SCALE * (preact + CUBIC_COEF * preact * preact * preact)
    tanh_part = jnp.tanh(inner)
    gelu_val = 0.5 * preact * (1.0 + tanh_part)
    gelu_slope = 0.5 * (1.0 + tanh_part) + 0.5 * preact * (
        1.0 - tanh_part * tanh_part
    ) * GELU_SCALE * (1.0 + 3.0 * CUBIC_COEF * preact * preact)
    return gelu_val, gelu_slope


def contract(left, right, left_axis, right_axis):
    return lax.dot_general(
        left, right, (((left_axis,), (right_axis,)), ((), ())), preferred_element_type=F32
    )


def onehot(base, chosen_row, tokens):
    rows = chosen_row.shape[1]
    ids = base + lax.broadcasted_iota(jnp.int32, (tokens, rows), 0)
    return jnp.where(ids == chosen_row, 1.0, 0.0).astype(BF)


def hi_lo(value):
    high = value.astype(BF)
    low = (value - high.astype(F32)).astype(BF)
    return high, low


def pick_kernel(
    base_ref, act_hbm, grad_hbm, chosen_hbm, out_ref, both_ref, chosen_ref, sems
):
    feats = act_hbm.shape[0]
    copies = [
        pltpu.make_async_copy(act_hbm, both_ref.at[pl.ds(0, feats)], sems.at[0]),
        pltpu.make_async_copy(grad_hbm, both_ref.at[pl.ds(feats, feats)], sems.at[1]),
        pltpu.make_async_copy(chosen_hbm, chosen_ref, sems.at[2]),
    ]
    for copy in copies:
        copy.start()
    for copy in copies:
        copy.wait()
    both = both_ref[...]
    for e in range(out_ref.shape[0]):
        sel = onehot(base_ref[0], chosen_ref[e : e + 1, :], both.shape[1])
        out_ref[e] = contract(both, sel, 1, 0).astype(BF)


def merge_kernel(parts_ref, out_ref):
    total = parts_ref[0].astype(F32)
    for k in range(1, parts_ref.shape[0]):
        total = total + parts_ref[k].astype(F32)
    total = total.astype(BF)
    for k in range(out_ref.shape[0]):
        out_ref[k] = total


def gate_tile(pairs):
    rows = [half.astype(F32) for pair in pairs for half in pair]
    rows.append(jnp.zeros((16 - len(rows), rows[0].shape[1]), F32))
    return jnp.concatenate(rows, axis=0).astype(BF)


def block_rows(slots_ref, slot, feats):
    return pl.ds(pl.multiple_of(slots_ref[slot] * feats, feats), feats)


def load_blocks(slots_ref, first, blocks_ref, x_ref, u_ref, x_sem, u_sem):
    outer, inner, both = blocks_ref.shape[:3]
    feats = both // 2
    for o in range(outer):
        for i in range(inner):
            at = block_rows(slots_ref, first + o * inner + i, feats)
            act, grad = (blocks_ref.at[o, i, pl.ds(h * feats, feats)] for h in range(2))
            pltpu.make_async_copy(act, x_ref.at[at], x_sem).start()
            pltpu.make_async_copy(grad, u_ref.at[at], u_sem).start()
    half = pl.ds(0, outer * inner * feats)
    return (
        pltpu.make_async_copy(x_ref.at[half], x_ref.at[half], x_sem),
        pltpu.make_async_copy(u_ref.at[half], u_ref.at[half], u_sem),
    )


def ready_kernel(
    slots_ref, own_ref, w_in_ref, x_ref, u_ref, turned_ref, order_ref, x_sem, u_sem
):
    arrived = load_blocks(slots_ref, 0, own_ref, x_ref, u_ref, x_sem, u_sem)
    turned_ref[...] = w_in_ref[...].T
    count, feats = slots_ref.shape[0] // 2, own_ref.shape[2] // 2
    for s in range(count):
        at = block_rows(slots_ref, count + s, feats)
        order_ref[pl.ds(s * feats, feats), :] = w_in_ref[at, :]
    for copy in arrived:
        copy.wait()


def more_kernel(slots_ref, oth_ref, pair_ref, x_in, u_in, x_ref, u_ref, x_sem, u_sem):
    count = pair_ref.shape[0] * pair_ref.shape[1]
    copies = []
    for k, ref in enumerate((oth_ref, pair_ref)):
        copies += load_blocks(slots_ref, (k + 1) * count, ref, x_ref, u_ref, x_sem.at[k], u_sem.at[k])
    for copy in copies:
        copy.wait()


def main_kernel(
    slots_ref, oth_ref, x_in, u_in, turned_ref, order_ref, w_out_ref, score_ref,
    x_ref, u_ref, back_ref, scaled_ref, gate_ref, send_ref, held_ref, x_sem, u_sem, w_sem,
):
    weights = pltpu.make_async_copy(w_out_ref, held_ref, w_sem)
    weights.start()
    count = oth_ref.shape[0] * oth_ref.shape[1]
    x_done, u_done = load_blocks(slots_ref, 3 * count, oth_ref, x_ref, u_ref, x_sem, u_sem)
    x_done.wait()
    preact = contract(turned_ref[...], x_ref[...], 1, 0)
    u_done.wait()
    weights.wait()
    raw = contract(held_ref[...], u_ref[...], 1, 0)
    val, slope = gelu_parts(preact)
    hidden = val.astype(BF).astype(F32)
    score = score_ref[...]
    gate = jnp.sum(hidden * raw, axis=0, keepdims=True)
    back = (score * raw * slope).astype(BF)
    back_ref[...] = back
    scaled_ref[...] = (score * hidden).astype(BF)
    gate_ref[...] = gate
    half = order_ref.shape[0] // 2
    send = contract(order_ref[pl.ds(half, half), :], back, 1, 0)
    send_ref[pl.ds(0, half), :] = send.astype(BF)
    send_ref[pl.ds(half, 16), :] = gate_tile([hi_lo(gate)])


def weight_kernel(x_ref, u_ref, back_ref, scaled_ref, gin_ref, gout_ref):
    gin_ref[...] = contract(x_ref[...], back_ref[...], 1, 1).astype(BF)
    gout_ref[...] = contract(scaled_ref[...], u_ref[...], 1, 1).astype(BF)


def pair_kernel(order_ref, back_ref, gate_ref, got_ref, out_ref):
    parts, rows = out_ref.shape[0], out_ref.shape[1] - 16
    back = back_ref[...]
    tile = got_ref[pl.ds(parts * rows, 16), :].astype(F32)
    high, low = hi_lo(gate_ref[...])
    gate = (high.astype(F32) + low.astype(F32)) + (tile[0:1] + tile[1:2])
    packed = gate_tile([hi_lo(gate)])
    for k in range(parts):
        at = pl.ds(k * rows, rows)
        mine = contract(order_ref[at, :], back, 1, 0)
        out_ref[k, :rows, :] = (mine + got_ref[at, :].astype(F32)).astype(BF)
        out_ref[k, rows:, :] = packed


def outer_kernel(got_ref, out_ref):
    count, rows = out_ref.shape[0], out_ref.shape[1] - 16
    base = count * rows
    tiles = [got_ref[o, pl.ds(base, 16), :].astype(F32) for o in range(4)]
    packed = gate_tile([(t[0:1], t[1:2]) for t in tiles])
    for i in range(count):
        at = pl.ds(i * rows, rows)
        total = got_ref[0, at, :].astype(F32)
        for o in range(1, 4):
            total = total + got_ref[o, at, :].astype(F32)
        out_ref[i, :rows, :] = total.astype(BF)
        out_ref[i, rows:, :] = packed


def inner_kernel(core_ref, got_ref, out_ref, gate_ref):
    rows = out_ref.shape[1]
    sources = got_ref.shape[0]
    total = got_ref[0, :rows, :].astype(F32)
    for i in range(1, sources):
        total = total + got_ref[i, :rows, :].astype(F32)
    total = total.astype(BF)
    for k in range(out_ref.shape[0]):
        out_ref[k] = total
    tiles = [got_ref[i, rows:, :].astype(F32) for i in range(sources)]
    gates = [[t[2 * o : 2 * o + 1] + t[2 * o + 1 : 2 * o + 2] for o in range(4)] for t in tiles]
    first = core_ref[0] == 0
    gate = jnp.zeros((1, got_ref.shape[2]), F32)
    for y in range(NY):
        for z in range(NZ):
            gate = gate + jnp.where(first, gates[y][z], gates[(y % 2) * NZ + z][y // 2])
    gate_ref[...] = gate


def scatter_kernel(base_ref, terms_ref, chosen_ref, out_ref):
    tokens = out_ref.shape[1]
    total = jnp.zeros(out_ref.shape, F32)
    for e in range(terms_ref.shape[0]):
        sel = onehot(base_ref[0], chosen_ref[e : e + 1, :], tokens)
        total = total + contract(terms_ref[e], sel, 1, 1)
    out_ref[...] = total.astype(BF)


SMEM = pl.BlockSpec(memory_space=pltpu.SMEM)
VMEM = pl.BlockSpec(memory_space=pltpu.VMEM)
HBM = pl.BlockSpec(memory_space=pltpu.HBM)
ANY = pl.BlockSpec(memory_space=pl.ANY)


def call(kernel, specs, outs, *args, scratch=(), alias=None, mib=16, flops=0, moved=0):
    shapes = [jax.ShapeDtypeStruct(s, t) for s, t in outs]
    single = len(shapes) == 1
    return pl.pallas_call(
        kernel,
        out_shape=shapes[0] if single else shapes,
        in_specs=specs,
        out_specs=VMEM if single else [VMEM] * len(shapes),
        scratch_shapes=scratch,
        input_output_aliases=alias or {},
        cost_estimate=pl.CostEstimate(flops=flops, bytes_accessed=moved, transcendentals=0),
        compiler_params=pltpu.CompilerParams(vmem_limit_bytes=mib * MIB),
    )(*args)


def in_hbm(value):
    return pltpu.with_memory_space_constraint(value, pltpu.HBM)


def exchange(parts, axis, groups=None):
    return lax.all_to_all(parts, axis, 0, 0, axis_index_groups=groups)


def block_table(core):
    o = jnp.arange(4, dtype=jnp.int32)[:, None]
    i = jnp.arange(8, dtype=jnp.int32)[None, :]
    zero = dp_index(i, o, 0)
    one = dp_index(2 * o + i // NZ, i % NZ, 1)
    return jnp.where(core == 0, zero, one).reshape(-1)


def half_table(core, parity):
    o = jnp.arange(4, dtype=jnp.int32)[:, None]
    i = jnp.arange(4, dtype=jnp.int32)[None, :]
    zero = dp_index(2 * i + parity, o, 0)
    one = dp_index(2 * o + parity, i, 1)
    return jnp.where(core == 0, zero, one).reshape(-1)


def per_device(activations, out_grad, w_in, w_out, chosen, gate_scores):
    tokens, feats = activations.shape
    experts, rows = chosen.shape
    depth, units = w_in.shape[1], w_in.shape[2]
    base = (lax.axis_index("expert") * tokens).astype(jnp.int32).reshape(1)
    index = lax.axis_index("dp").astype(jnp.int32)
    core, parity = index & 1, (index >> 3) & 1
    slots = jnp.concatenate(
        [
            half_table(core, parity),
            half_table(1 - core, parity),
            half_table(core, 1 - parity),
            half_table(1 - core, 1 - parity),
            block_table(core),
            block_table(1 - core),
        ]
    )
    count = slots.shape[0] // 4

    picked = call(
        pick_kernel,
        [SMEM, HBM, HBM, HBM],
        [((experts, 2 * feats, rows), BF)],
        base, in_hbm(activations.T), in_hbm(out_grad.T), in_hbm(chosen),
        scratch=[
            pltpu.VMEM((2 * feats, tokens), BF),
            pltpu.VMEM((experts, rows), jnp.int32),
            pltpu.SemaphoreType.DMA((3,)),
        ],
    )
    picked = exchange(picked, "expert")
    mine = call(merge_kernel, [VMEM], [((4, 2 * feats, rows), BF)], picked)
    first = exchange(mine, "dp", FIRST)
    own = exchange(jnp.broadcast_to(first[None], (4,) + first.shape), "dp", SECOND)
    pair = lax.ppermute(own, "dp", NEIGHBOUR)
    near = lax.ppermute(own, "dp", SWAP)
    sems = [pltpu.SemaphoreType.DMA] * 2
    held = [((depth, rows), BF), ((depth, rows), BF)]
    weight = ((depth, units), BF)
    x, u, turned, order = call(
        ready_kernel, [SMEM, ANY, VMEM], held + [((units, depth), BF), weight],
        slots, own, w_in[0],
        scratch=sems, flops=2 * MIB, moved=6 * MIB,
    )
    near, pair, x, u, turned = lax.optimization_barrier((near, pair, x, u, turned))
    other = lax.ppermute(pair, "dp", SWAP)
    x, u = call(
        more_kernel, [SMEM, ANY, ANY, VMEM, VMEM], held, slots, in_hbm(near), pair, x, u,
        scratch=[pltpu.SemaphoreType.DMA((2,))] * 2, alias={3: 0, 4: 1},
        flops=2 * MIB, moved=3 * MIB,
    )
    x, u, back, scaled, gate, send = call(
        main_kernel,
        [SMEM, ANY] + [VMEM] * 4 + [HBM, VMEM],
        held
        + [
            ((units, rows), BF),
            ((units, rows), BF),
            ((1, rows), F32),
            ((count * feats + 16, rows), BF),
        ],
        slots, other, x, u, turned, order, in_hbm(w_out[0]), gate_scores,
        scratch=[pltpu.VMEM((units, depth), BF)] + [pltpu.SemaphoreType.DMA] * 3, alias={2: 0, 3: 1},
    )
    got = lax.ppermute(send, "dp", SWAP)
    weight_grads = call(
        weight_kernel,
        [VMEM] * 4,
        [((depth, units), BF), ((units, depth), BF)],
        x, u, back, scaled, flops=4 * depth * units * rows, moved=6 * depth * rows,
    )
    got, weight_in_grad, weight_out_grad = lax.optimization_barrier((got, *weight_grads))
    part = call(
        pair_kernel,
        [VMEM] * 4,
        [((4, 8 * feats + 16, rows), BF)],
        order, back, gate, got,
    )
    part = exchange(part, "dp", OUTER)
    part = call(outer_kernel, [VMEM], [((8, feats + 16, rows), BF)], part)
    part = exchange(part, "dp", INNER)
    term, gate_grad = call(
        inner_kernel, [SMEM, VMEM], [((experts, feats, rows), BF), ((1, rows), F32)],
        core.reshape(1), part,
    )
    terms = exchange(term, "expert")
    act_grad = call(
        scatter_kernel, [SMEM, VMEM, VMEM], [((feats, tokens), BF)], base, terms, chosen
    )
    return weight_in_grad[None], weight_out_grad[None], act_grad.T, gate_grad


def solution(mesh):
    return jax.shard_map(
        per_device,
        mesh=mesh,
        in_specs=(
            P("expert", "dp"),
            P("expert", "dp"),
            P("expert", None, "dp"),
            P("expert", "dp", None),
            P(),
            P("expert", None),
        ),
        out_specs=(
            P("expert", None, "dp"),
            P("expert", "dp", None),
            P("expert", "dp"),
            P("expert", None),
        ),
        check_vma=False,
    )
```
